128 devices in a mesh: dp: 2 (over x_hi), expert: 64 (over z, x_lo, y, core).
Axes of the slice: x: 4 (x_hi: 2, x_lo: 2; x = x_hi * 2 + x_lo), y: 4, z: 4, core: 2. Of those that a mesh axis runs over, the one named last changes fastest.
Arguments:
- tokens: bfloat16 [16384, 2048], P(('dp', 'expert')), may hold values from -6 to 6
- routes: int32 [16384, 4], P(('dp', 'expert')), may hold values from 0 to 63, all different within a row; in each aligned block of 128 rows (0 to 127, 128 to 255, ...) at most 16 rows name the same one
- route_gates: bfloat16 [16384, 4], P(('dp', 'expert')), may hold values from 0.049804688 to 1
- cotangent: bfloat16 [16384, 2048], P(('dp', 'expert')), may hold values from -3 to 3
- swap_pairs: int32 [32, 2], replicated, may hold values from 0 to 63, as said below
- w_gate: bfloat16 [64, 2048, 768], P('expert'), may hold values from -0.125 to 0.125
- w_up: bfloat16 [64, 2048, 768], P('expert'), may hold values from -0.125 to 0.125
- w_down: bfloat16 [64, 768, 2048], P('expert'), may hold values from -0.21875 to 0.21875
- moment_first: bfloat16 [64, 768, 2048], P('expert', 'dp'), may hold values from -6 to 6
- moment_second: bfloat16 [64, 768, 2048], P('expert', 'dp'), may hold values from 0.099609375 to 4
Outputs:
- combined: bfloat16 [16384, 2048], P(('dp', 'expert'))
- new_gate: bfloat16 [64, 2048, 768], P('expert', None, 'dp')
- new_up: bfloat16 [64, 2048, 768], P('expert', None, 'dp')
- new_down: bfloat16 [64, 768, 2048], P('expert', 'dp')
- new_first: bfloat16 [64, 768, 2048], P('expert', 'dp')
- new_second: bfloat16 [64, 768, 2048], P('expert', 'dp')
- adam_step: bfloat16 [64, 768, 2048], P('expert', 'dp')
The draws below stay inside these ranges and needn't reach their ends.
Inputs may be any that keep to these rules, and one draw needn't show every extreme that they name: `routes`: each aligned block of 128 tokens (the tokens of one device) names no expert more than 16 times, and some block names some expert exactly 16 times; each token names 4 different experts. `swap_pairs`: every device index of the expert axis appears exactly once, so every device trades its expert with one other.
All inputs are finite; a program needn't handle non-finite values.
Results may differ from the reference program's by a relative error of at most 0.014.
Values may be sent and summed in bfloat16 or wider, within the bound.
No kernel may reach another device: no remote copies, remote signals or barrier semaphores. Data moves between devices by JAX's collectives and lax.ppermute only.
A program may use at most 192 MiB of HBM per device.

```python
import math
import jax
import jax.numpy as jnp
import numpy as np
from jax import lax

D = 2048
FF = 768
TOP = 4
TOK_DEV = 128
EXPERTS = 64
PAIRS = 32
CAP = 16
TOKENS = 16384
N_DP = 2
N_EXPERT = 64


def draw_swap_pairs(key, part):
    shuffled = jax.random.permutation(key, EXPERTS)
    return shuffled.reshape(PAIRS, 2).astype(jnp.int32)


def steps_of(key, dims, shards, least, largest):
    def one(axis_at, parts):
        draws = jax.random.uniform(jax.random.fold_in(jax.random.fold_in(key, 6), axis_at), (parts,), jnp.float32, least / len(shards), largest / len(shards))
        return jnp.repeat(jnp.exp(draws), dims[axis_at] // parts).reshape((-1,) + (1,) * (len(dims) - axis_at - 1))

    factor_of = one(*shards[0])
    for cut in shards[1:]:
        factor_of = factor_of * one(*cut)
    return factor_of


def shared_out(key, own, number, rows, count, top, bound, slope):
    order = jax.random.permutation(key, count)
    packed, usual = shares(count, rows * top, bound, slope, True), shares(count, rows * top, bound, slope, False)
    places = jnp.arange(count)

    def named(lengths, turn):
        used = int((lengths > 0).sum())
        fixed = max(1, used // 4)
        shifted = fixed + (places - fixed + turn * (used - fixed)) % max(1, count - fixed)
        return jnp.zeros((count,), jnp.int32).at[order[jnp.where(places < fixed, places, shifted)]].set(jnp.asarray(lengths, jnp.int32))

    lengths = jnp.where(number % 4 == 0, named(packed, number // 4), named(usual, number - number // 4 - 1))
    mixed = jax.random.permutation(jax.random.fold_in(own, 3), count)
    giver, taker = mixed[0:count // 2 * 2:2], mixed[1:count // 2 * 2:2]
    margin = jnp.minimum(lengths[giver] - 1, bound - lengths[taker]) // 2
    margin = jnp.where((giver == order[0]) | (taker == order[0]) | (lengths[taker] == 0), 0, jnp.maximum(margin, 0))
    shifted = jax.random.randint(jax.random.fold_in(own, 4), (count // 2,), 0, 1 << 20) % (margin + 1)
    lengths = lengths.at[giver].add(-shifted).at[taker].add(shifted)
    members = jnp.searchsorted(jnp.cumsum(lengths), jnp.arange(rows * top), side="right").astype(jnp.int32)
    listing = members.reshape(top, rows).T
    listing = listing[jax.random.permutation(jax.random.fold_in(own, 1), rows)]
    turn = jax.random.randint(jax.random.fold_in(own, 2), (rows, 1), 0, top)
    return jnp.take_along_axis(listing, (jnp.arange(top)[None, :] + turn) % top, axis=1)


def shares(number_of, total, bound, lean, full):
    weights = [(1 << 20) // math.isqrt(rank ** lean) + 1 for rank in range(1, number_of + 1)]
    largest = bound if full else min(bound, max(-(-total // number_of), total * weights[0] // sum(weights)))
    least = 1 if total - largest >= number_of - 1 else 0
    holding, spare = [largest] + [least] * (number_of - 1), total - largest - least * (number_of - 1)
    while spare > 0:
        candidates = [i for i in range(1, number_of) if holding[i] < largest] or [i for i in range(1, number_of) if holding[i] < bound]
        mass, left = sum([weights[i] for i in candidates]), spare
        for i in candidates:
            more = min(bound - holding[i], max(1, left * weights[i] // mass), spare)
            holding[i] = holding[i] + more
            spare = spare - more
    return np.array(holding)


def scatter_about(stream_key, extent, width, limit, split=(), kind=jnp.bfloat16):
    values = width * jax.random.normal(stream_key, extent, jnp.float32)
    if split:
        values = values * steps_of(stream_key, extent, split, -0.22, 0.18)
    return jnp.clip(values, -limit, limit).astype(kind)


def setup_inputs(seed: int = 0) -> dict:
    key_of = jax.random.split(jax.random.key(seed), 11)
    tokens = scatter_about(key_of[0], (TOKENS, D), 1.0, 6.0, ((0, 128),))
    routes_keys = jax.random.split(jax.random.fold_in(key_of[1], 1), TOKENS // TOK_DEV)
    routes_turns = jax.random.permutation(jax.random.fold_in(key_of[1], 3), TOKENS // TOK_DEV)
    routes = jax.vmap(lambda own, number: shared_out(jax.random.fold_in(key_of[1], 2), own, number, TOK_DEV, EXPERTS, TOP, CAP, 1))(routes_keys, routes_turns).reshape((TOKENS, TOP))
    route_gates = jnp.clip(jnp.exp(math.log(1.0) - 2.9996462 * jax.random.uniform(key_of[2], (TOKENS, TOP), jnp.float32) ** steps_of(key_of[2], (TOKENS, TOP), ((0, 128),), -0.2, 0.2)), 0.049804688, 1.0).astype(jnp.bfloat16)
    cotangent = scatter_about(key_of[3], (TOKENS, D), 0.5, 3.0, ((0, 128),))
    swap_pairs = draw_swap_pairs(jax.random.fold_in(key_of[10], 71), 0)
    w_gate = scatter_about(key_of[5], (EXPERTS, D, FF), D ** -0.5, 0.125, ((0, 64),))
    w_up = scatter_about(key_of[6], (EXPERTS, D, FF), D ** -0.5, 0.125, ((0, 64),))
    w_down = scatter_about(key_of[7], (EXPERTS, FF, D), FF ** -0.5, 0.21875, ((0, 64),))
    moment_first = scatter_about(key_of[8], (EXPERTS, FF, D), 1.0, 6.0, ((0, 64), (1, 2)))
    moment_second = jnp.clip(jnp.exp(math.log(4.0) - 3.6927934 * jax.random.uniform(key_of[9], (EXPERTS, FF, D), jnp.float32) ** steps_of(key_of[9], (EXPERTS, FF, D), ((0, 64), (1, 2)), -0.2, 0.2)), 0.099609375, 4.0).astype(jnp.bfloat16)
    return dict(tokens=tokens, routes=routes, route_gates=route_gates, cotangent=cotangent, swap_pairs=swap_pairs, w_gate=w_gate, w_up=w_up, w_down=w_down, moment_first=moment_first, moment_second=moment_second)


beta_first = 0.9
beta_second = 0.95
adam_eps = 1e-08

def partners(swap_pairs, count):
    slot_ids = jnp.arange(count, dtype=jnp.int32)
    pair_left = swap_pairs[:, 0:1]
    pair_right = swap_pairs[:, 1:2]
    offsets = jnp.where(pair_left == slot_ids[None, :], pair_right - slot_ids[None, :], 0)
    offsets = offsets + jnp.where(pair_right == slot_ids[None, :], pair_left - slot_ids[None, :], 0)
    return (slot_ids + lax.optimization_barrier(jnp.sum(offsets, axis=0))).astype(jnp.int32)

def expert_rows(x_rep, dy_rep, route_rep, gate_rep, expert, gate_e, up_e, down_e):
    is_hit = route_rep == expert
    token_hit = jnp.any(is_hit, axis=1)
    weight_e = lax.optimization_barrier(jnp.sum(jnp.where(is_hit, gate_rep.astype(jnp.float32), 0.0), axis=1))
    row_order = jnp.argsort(jnp.where(token_hit, 0, 1).astype(jnp.int32), stable=True)[:N_EXPERT * CAP]
    row_order = row_order.astype(jnp.int32)
    is_valid = token_hit[row_order]
    rows_x = x_rep[row_order].astype(jnp.float32)
    gate_pre = jnp.dot(rows_x, gate_e, precision=lax.Precision.HIGHEST)
    up_pre = jnp.dot(rows_x, up_e, precision=lax.Precision.HIGHEST)
    hidden = (jax.nn.silu(gate_pre) * up_pre).astype(jnp.bfloat16)
    hidden_f = hidden.astype(jnp.float32)
    outputs = jnp.dot(hidden_f, down_e, precision=lax.Precision.HIGHEST).astype(jnp.bfloat16)
    weight_row = jnp.where(is_valid, weight_e[row_order], 0.0)
    scaled = (weight_row[:, None] * dy_rep[row_order].astype(jnp.float32)).astype(jnp.bfloat16)
    partial_value = jnp.dot(hidden_f.T, scaled.astype(jnp.float32), precision=lax.Precision.HIGHEST)
    contrib = weight_row[:, None] * outputs.astype(jnp.float32)
    return (row_order, contrib, partial_value.astype(jnp.bfloat16))

def reference(tokens, routes, route_gates, cotangent, swap_pairs, w_gate, w_up, w_down, moment_first, moment_second):
    per_rep = N_EXPERT * TOK_DEV
    x_all = tokens.reshape(N_DP, per_rep, D)
    dy_all = cotangent.reshape(N_DP, per_rep, D)
    route_all = routes.reshape(N_DP, per_rep, TOP)
    gate_all = route_gates.reshape(N_DP, per_rep, TOP)

    def one_expert(totals, expert):
        gate_e = lax.dynamic_index_in_dim(w_gate, expert, 0, keepdims=False).astype(jnp.float32)
        up_e = lax.dynamic_index_in_dim(w_up, expert, 0, keepdims=False).astype(jnp.float32)
        down_e = lax.dynamic_index_in_dim(w_down, expert, 0, keepdims=False).astype(jnp.float32)
        grad_sum = jnp.zeros((FF, D), jnp.float32)
        updated = []
        for replica in range(N_DP):
            row_order, contrib, partial_value = expert_rows(x_all[replica], dy_all[replica], route_all[replica], gate_all[replica], expert, gate_e, up_e, down_e)
            updated.append(totals[replica].at[row_order].add(contrib))
            grad_sum = grad_sum + partial_value.astype(jnp.float32)
        return (jnp.stack(updated), grad_sum)
    start_totals = jnp.zeros((N_DP, per_rep, D), jnp.float32)
    totals, grads = lax.scan(one_expert, start_totals, jnp.arange(EXPERTS, dtype=jnp.int32))
    first_moment = beta_first * moment_first.astype(jnp.float32) + (1.0 - beta_first) * grads
    second_moment = beta_second * moment_second.astype(jnp.float32) + (1.0 - beta_second) * grads * grads
    direction = first_moment / (jnp.sqrt(second_moment) + adam_eps)
    partner = partners(swap_pairs, EXPERTS)
    combined = totals.reshape(TOKENS, D).astype(jnp.bfloat16)
    return (combined, w_gate[partner], w_up[partner], w_down[partner], first_moment.astype(jnp.bfloat16)[partner], second_moment.astype(jnp.bfloat16)[partner], direction.astype(jnp.bfloat16)[partner])
```

```python
import jax
import jax.numpy as jnp
from jax import lax
from jax.sharding import PartitionSpec as P

beta_first = 0.9
beta_second = 0.95
adam_eps = 1e-08
capacity = 16


def partners(swap_pairs, count):
    slot_ids = jnp.arange(count, dtype=jnp.int32)
    pair_left = swap_pairs[:, 0:1]
    pair_right = swap_pairs[:, 1:2]
    offsets = jnp.where(pair_left == slot_ids[None, :], pair_right - slot_ids[None, :], 0)
    offsets = offsets + jnp.where(pair_right == slot_ids[None, :], pair_left - slot_ids[None, :], 0)
    return slot_ids + jnp.sum(offsets, axis=0)


def to_tiles(array, pieces):
    rows, columns = array.shape
    tiles = array.reshape(rows // 8, 8, columns // 128, 128).transpose(0, 2, 1, 3)
    return tiles.reshape(pieces, -1, 8, 128)


def from_tiles(tiles, rows, columns):
    split = tiles.reshape(rows // 8, columns // 128, 8, 128).transpose(0, 2, 1, 3)
    return split.reshape(rows, columns)


def exchange(array):
    return lax.all_to_all(array, "expert", split_axis=0, concat_axis=0, tiled=True)


def adam_update(first_in, second_in, grad):
    first_moment = beta_first * first_in.astype(jnp.float32) + (1.0 - beta_first) * grad
    second_moment = beta_second * second_in.astype(jnp.float32) + (1.0 - beta_second) * grad * grad
    direction = first_moment / (jnp.sqrt(second_moment) + adam_eps)
    return (
        first_moment.astype(jnp.bfloat16),
        second_moment.astype(jnp.bfloat16),
        direction.astype(jnp.bfloat16),
    )


def slots(routes, route_gates, count):
    tok = routes.shape[0]
    expert_ids = jnp.arange(count, dtype=jnp.int32)
    hits = routes.T[:, None, :] == expert_ids[None, :, None]
    named = jnp.any(hits, axis=0)
    weight = jnp.sum(
        jnp.where(hits, route_gates.T.astype(jnp.float32)[:, None, :], 0.0), axis=0
    )
    earlier = (
        jnp.arange(tok, dtype=jnp.int32)[:, None] < jnp.arange(tok, dtype=jnp.int32)[None, :]
    ).astype(jnp.bfloat16)
    rank = jnp.dot(
        named.astype(jnp.bfloat16), earlier, preferred_element_type=jnp.float32
    ).astype(jnp.int32)
    slot_ids = jnp.arange(capacity, dtype=jnp.int32)
    chosen = named[:, None, :] & (rank[:, None, :] == slot_ids[None, :, None])
    pick = chosen.astype(jnp.bfloat16)
    weigh = jnp.where(chosen, weight[:, None, :], 0.0).astype(jnp.bfloat16)
    return pick, weigh


def local(
    tokens,
    routes,
    route_gates,
    cotangent,
    swap_pairs,
    w_gate,
    w_up,
    w_down,
    moment_first,
    moment_second,
):
    count = lax.axis_size("expert")
    replica = lax.axis_index("dp")
    tok, width = tokens.shape
    partner = partners(swap_pairs, count)
    gate_w, up_w, down_w = w_gate[0], w_up[0], w_down[0]
    ff = gate_w.shape[1]
    half = ff // lax.axis_size("dp")

    pick, weigh = slots(routes, route_gates, count)
    blank = jnp.zeros_like(pick)
    both = jnp.concatenate(
        [jnp.concatenate([pick, blank], axis=2), jnp.concatenate([blank, weigh], axis=2)], axis=1
    )
    rows_out = jnp.dot(
        both.reshape(count * 2 * capacity, 2 * tok),
        jnp.concatenate([tokens, cotangent], axis=0),
        preferred_element_type=jnp.float32,
    ).astype(jnp.bfloat16)
    rows_in = exchange(rows_out.reshape(count, 2 * capacity, width))

    gate_half = lax.dynamic_slice_in_dim(gate_w, replica * half, half, 1)
    up_half = lax.dynamic_slice_in_dim(up_w, replica * half, half, 1)
    down_half = lax.dynamic_slice_in_dim(down_w, replica * half, half, 0)
    state = jnp.concatenate(
        [
            to_tiles(member, count)
            for member in (gate_half, up_half, down_half, moment_first[0], moment_second[0])
        ],
        axis=1,
    )
    state, rows_in = lax.optimization_barrier((state, rows_in))
    spread = exchange(state)

    x_rows = rows_in[:, :capacity].reshape(count * capacity, width)
    scaled = rows_in[:, capacity:].reshape(count * capacity, width)
    gate_pre = jnp.dot(x_rows, gate_w, preferred_element_type=jnp.float32)
    up_pre = jnp.dot(x_rows, up_w, preferred_element_type=jnp.float32)
    hidden = (jax.nn.silu(gate_pre) * up_pre).astype(jnp.bfloat16)
    partial = lax.dot_general(
        hidden, scaled, (((0,), (0,)), ((), ())), preferred_element_type=jnp.float32
    ).astype(jnp.bfloat16)
    kept = lax.dynamic_slice_in_dim(partial, replica * half, half, 0)
    given = lax.dynamic_slice_in_dim(partial, (1 - replica) * half, half, 0)
    taken = lax.ppermute(given, "dp", [(0, 1), (1, 0)])
    outputs = jnp.dot(hidden, down_w, preferred_element_type=jnp.float32).astype(jnp.bfloat16)
    grad = (kept.astype(jnp.float32) + taken.astype(jnp.float32)).astype(jnp.bfloat16)
    answer = jnp.concatenate([to_tiles(outputs, count), to_tiles(grad, count)], axis=1)
    answer, spread = lax.optimization_barrier((answer, spread))
    answered = exchange(answer)

    out_tiles = 2 * (width // 128)
    returned = from_tiles(answered[:, :out_tiles], count * capacity, width)
    combined = lax.dot_general(
        weigh.reshape(count * capacity, tok),
        returned,
        (((0,), (0,)), ((), ())),
        preferred_element_type=jnp.float32,
    ).astype(jnp.bfloat16)

    onward = jnp.concatenate([spread, answered[:, out_tiles:]], axis=1)[partner]
    landed = exchange(onward)

    share = half * width // (count * 8 * 128)
    gate_out, up_out, down_out, first_in, second_in, grad_in = [
        landed[:, i * share : (i + 1) * share] for i in range(6)
    ]
    first_out, second_out, step_out = adam_update(
        from_tiles(first_in, half, width),
        from_tiles(second_in, half, width),
        from_tiles(grad_in, half, width).astype(jnp.float32),
    )
    return (
        combined,
        from_tiles(gate_out, width, half)[None],
        from_tiles(up_out, width, half)[None],
        from_tiles(down_out, half, width)[None],
        first_out[None],
        second_out[None],
        step_out[None],
    )


def solution(mesh):
    placed = (
        P(("dp", "expert"), None),
        P(("dp", "expert"), None),
        P(("dp", "expert"), None),
        P(("dp", "expert"), None),
        P(),
        P("expert", None, None),
        P("expert", None, None),
        P("expert", None, None),
        P("expert", "dp", None),
        P("expert", "dp", None),
    )
    return jax.shard_map(
        local,
        mesh=mesh,
        in_specs=placed,
        out_specs=(
            P(("dp", "expert"), None),
            P("expert", None, "dp"),
            P("expert", None, "dp"),
            P("expert", "dp", None),
            P("expert", "dp", None),
            P("expert", "dp", None),
            P("expert", "dp", None),
        ),
        check_vma=False,
    )
```

```python
import jax
import jax.numpy as jnp
from jax import lax
from jax.sharding import PartitionSpec as P

beta_first = 0.9
beta_second = 0.95
adam_eps = 1e-08
capacity = 16


def partners(swap_pairs, count):
    slot_ids = jnp.arange(count, dtype=jnp.int32)
    pair_left = swap_pairs[:, 0:1]
    pair_right = swap_pairs[:, 1:2]
    offsets = jnp.where(pair_left == slot_ids[None, :], pair_right - slot_ids[None, :], 0)
    offsets = offsets + jnp.where(pair_right == slot_ids[None, :], pair_left - slot_ids[None, :], 0)
    return slot_ids + jnp.sum(offsets, axis=0)


def to_tiles(array, pieces):
    rows, columns = array.shape
    tiles = array.reshape(rows // 8, 8, columns // 128, 128).transpose(0, 2, 1, 3)
    return tiles.reshape(pieces, -1, 8, 128)


def from_tiles(tiles, rows, columns):
    split = tiles.reshape(rows // 8, columns // 128, 8, 128).transpose(0, 2, 1, 3)
    return split.reshape(rows, columns)


def exchange(array):
    return lax.all_to_all(array, "expert", split_axis=0, concat_axis=0, tiled=True)


def adam_update(first_in, second_in, grad):
    first_moment = beta_first * first_in.astype(jnp.float32) + (1.0 - beta_first) * grad
    second_moment = beta_second * second_in.astype(jnp.float32) + (1.0 - beta_second) * grad * grad
    direction = first_moment / (jnp.sqrt(second_moment) + adam_eps)
    return (
        first_moment.astype(jnp.bfloat16),
        second_moment.astype(jnp.bfloat16),
        direction.astype(jnp.bfloat16),
    )


def slots(routes, route_gates, count):
    tok = routes.shape[0]
    expert_ids = jnp.arange(count, dtype=jnp.int32)
    hits = routes.T[:, None, :] == expert_ids[None, :, None]
    named = jnp.any(hits, axis=0)
    weight = jnp.sum(
        jnp.where(hits, route_gates.T.astype(jnp.float32)[:, None, :], 0.0), axis=0
    )
    earlier = (
        jnp.arange(tok, dtype=jnp.int32)[:, None] < jnp.arange(tok, dtype=jnp.int32)[None, :]
    ).astype(jnp.bfloat16)
    rank = jnp.dot(
        named.astype(jnp.bfloat16), earlier, preferred_element_type=jnp.float32
    ).astype(jnp.int32)
    slot_ids = jnp.arange(capacity, dtype=jnp.int32)
    chosen = named[:, None, :] & (rank[:, None, :] == slot_ids[None, :, None])
    pick = chosen.astype(jnp.bfloat16)
    weigh = jnp.where(chosen, weight[:, None, :], 0.0).astype(jnp.bfloat16)
    return pick, weigh


def local(
    tokens,
    routes,
    route_gates,
    cotangent,
    swap_pairs,
    w_gate,
    w_up,
    w_down,
    moment_first,
    moment_second,
):
    count = lax.axis_size("expert")
    replica = lax.axis_index("dp")
    tok, width = tokens.shape
    partner = partners(swap_pairs, count)
    gate_w, up_w, down_w = w_gate[0], w_up[0], w_down[0]
    ff = gate_w.shape[1]
    half = ff // lax.axis_size("dp")

    pick, weigh = slots(routes, route_gates, count)
    blank = jnp.zeros_like(pick)
    both = jnp.concatenate(
        [jnp.concatenate([pick, blank], axis=2), jnp.concatenate([blank, weigh], axis=2)], axis=1
    )
    rows_out = jnp.dot(
        both.reshape(count * 2 * capacity, 2 * tok),
        jnp.concatenate([tokens, cotangent], axis=0),
        preferred_element_type=jnp.float32,
    ).astype(jnp.bfloat16)
    rows_in = exchange(rows_out.reshape(count, 2 * capacity, width))

    gate_half = lax.dynamic_slice_in_dim(gate_w, replica * half, half, 1)
    up_half = lax.dynamic_slice_in_dim(up_w, replica * half, half, 1)
    down_half = lax.dynamic_slice_in_dim(down_w, replica * half, half, 0)
    state = jnp.concatenate(
        [
            to_tiles(member, count)
            for member in (gate_half, up_half, down_half, moment_first[0], moment_second[0])
        ],
        axis=1,
    )
    state, rows_in = lax.optimization_barrier((state, rows_in))
    spread = exchange(state)

    x_rows = rows_in[:, :capacity].reshape(count * capacity, width)
    scaled = rows_in[:, capacity:].reshape(count * capacity, width)
    gate_pre = jnp.dot(x_rows, gate_w, preferred_element_type=jnp.float32)
    up_pre = jnp.dot(x_rows, up_w, preferred_element_type=jnp.float32)
    hidden = (jax.nn.silu(gate_pre) * up_pre).astype(jnp.bfloat16)
    partial = lax.dot_general(
        hidden, scaled, (((0,), (0,)), ((), ())), preferred_element_type=jnp.float32
    ).astype(jnp.bfloat16)
    outputs = jnp.dot(hidden, down_w, preferred_element_type=jnp.float32).astype(jnp.bfloat16)
    pieces = to_tiles(partial, lax.axis_size("dp") * count)
    pieces, spread = lax.optimization_barrier((pieces, spread))
    halves = lax.all_to_all(pieces, ("dp", "expert"), split_axis=0, concat_axis=0, tiled=True)

    answer = to_tiles(outputs, count)
    moved = spread[partner]
    share = moved.shape[1] // 5
    onward = jnp.concatenate([answer, moved, moved[:, :share]], axis=1)
    onward, halves = lax.optimization_barrier((onward, halves))
    grad = jnp.sum(halves.reshape(-1, count, share, 8, 128).astype(jnp.float32), axis=0)
    grad = grad.astype(jnp.bfloat16)[partner]
    out_tiles = answer.shape[1]
    onward = lax.dynamic_update_slice(onward, grad, (0, out_tiles + 5 * share, 0, 0))
    landed = exchange(onward)

    returned = from_tiles(landed[:, :out_tiles], count * capacity, width)
    combined = lax.dot_general(
        weigh.reshape(count * capacity, tok),
        returned,
        (((0,), (0,)), ((), ())),
        preferred_element_type=jnp.float32,
    ).astype(jnp.bfloat16)
    gate_out, up_out, down_out, first_in, second_in, grad_in = [
        landed[:, out_tiles + i * share : out_tiles + (i + 1) * share] for i in range(6)
    ]
    first_out, second_out, step_out = [
        from_tiles(member, half, width)
        for member in adam_update(first_in, second_in, grad_in.astype(jnp.float32))
    ]
    return (
        combined,
        from_tiles(gate_out, width, half)[None],
        from_tiles(up_out, width, half)[None],
        from_tiles(down_out, half, width)[None],
        first_out[None],
        second_out[None],
        step_out[None],
    )


def solution(mesh):
    placed = (
        P(("dp", "expert"), None),
        P(("dp", "expert"), None),
        P(("dp", "expert"), None),
        P(("dp", "expert"), None),
        P(),
        P("expert", None, None),
        P("expert", None, None),
        P("expert", None, None),
        P("expert", "dp", None),
        P("expert", "dp", None),
    )
    return jax.shard_map(
        local,
        mesh=mesh,
        in_specs=placed,
        out_specs=(
            P(("dp", "expert"), None),
            P("expert", None, "dp"),
            P("expert", None, "dp"),
            P("expert", "dp", None),
            P("expert", "dp", None),
            P("expert", "dp", None),
            P("expert", "dp", None),
        ),
        check_vma=False,
    )
```

```python
import jax
import jax.numpy as jnp
from jax import lax
from jax.experimental import pallas as pl
from jax.experimental.pallas import tpu as pltpu
from jax.sharding import PartitionSpec as P

beta_first = 0.9
beta_second = 0.95
adam_eps = 1e-08
capacity = 16


def partners(swap_pairs, count):
    slot_ids = jnp.arange(count, dtype=jnp.int32)
    pair_left = swap_pairs[:, 0:1]
    pair_right = swap_pairs[:, 1:2]
    offsets = jnp.where(pair_left == slot_ids[None, :], pair_right - slot_ids[None, :], 0)
    offsets = offsets + jnp.where(pair_right == slot_ids[None, :], pair_left - slot_ids[None, :], 0)
    return slot_ids + jnp.sum(offsets, axis=0)


def to_tiles(array, pieces):
    rows, columns = array.shape
    tiles = array.reshape(rows // 8, 8, columns // 128, 128).transpose(0, 2, 1, 3)
    return tiles.reshape(pieces, -1, 8, 128)


def from_tiles(tiles, rows, columns):
    split = tiles.reshape(rows // 8, columns // 128, 8, 128).transpose(0, 2, 1, 3)
    return split.reshape(rows, columns)


def exchange(array):
    return lax.all_to_all(array, "expert", split_axis=0, concat_axis=0, tiled=True)


def adam_update(first_in, second_in, grad):
    first_moment = beta_first * first_in.astype(jnp.float32) + (1.0 - beta_first) * grad
    second_moment = beta_second * second_in.astype(jnp.float32) + (1.0 - beta_second) * grad * grad
    direction = first_moment / (jnp.sqrt(second_moment) + adam_eps)
    return (
        first_moment.astype(jnp.bfloat16),
        second_moment.astype(jnp.bfloat16),
        direction.astype(jnp.bfloat16),
    )


def pack_kernel(
    replica_ref,
    routes_ref,
    gates_ref,
    tokens_ref,
    cotangent_ref,
    gate_ref,
    up_ref,
    down_ref,
    first_ref,
    second_ref,
    out_ref,
    weigh_ref,
    rank_ref,
    weight_ref,
):
    count, tok = rank_ref.shape
    dests = out_ref.shape[0]
    step = pl.program_id(0)

    @pl.when(step == 0)
    def _():
        expert_ids = lax.broadcasted_iota(jnp.int32, (count, tok), 0)
        named = jnp.zeros((count, tok), jnp.float32)
        weight = jnp.zeros((count, tok), jnp.float32)
        for k in range(routes_ref.shape[0]):
            hit = routes_ref[k : k + 1, :] == expert_ids
            named = jnp.where(hit, 1.0, named)
            weight = jnp.where(hit, gates_ref[k : k + 1, :], weight)
        earlier = lax.broadcasted_iota(jnp.int32, (tok, tok), 0) < lax.broadcasted_iota(
            jnp.int32, (tok, tok), 1
        )
        rank = jnp.dot(
            named.astype(jnp.bfloat16),
            jnp.where(earlier, 1.0, 0.0).astype(jnp.bfloat16),
            preferred_element_type=jnp.float32,
        )
        rank_ref[...] = jnp.where(named > 0.0, rank, -1.0)
        weight_ref[...] = weight

    here = pl.ds(pl.multiple_of(step * dests, dests), dests)
    rank = rank_ref[here, :]
    weight = weight_ref[here, :]
    slot_ids = lax.broadcasted_iota(jnp.int32, (capacity, tok), 0).astype(jnp.float32)
    picks, weighs = [], []
    for s in range(dests):
        chosen = rank[s : s + 1, :] == slot_ids
        picks.append(jnp.where(chosen, 1.0, 0.0))
        weighs.append(jnp.where(chosen, weight[s : s + 1, :], 0.0))
    pick = jnp.concatenate(picks, axis=0).astype(jnp.bfloat16)
    weigh = jnp.concatenate(weighs, axis=0).astype(jnp.bfloat16)
    weigh_ref[...] = weigh
    x_rows = jnp.dot(pick, tokens_ref[...], preferred_element_type=jnp.float32)
    scaled = jnp.dot(weigh, cotangent_ref[...], preferred_element_type=jnp.float32)

    def spread(source, first_slot):
        tall, wide = source.shape[0] // 8, source.shape[1] // 128
        each = tall * wide // dests
        for index in range(tall * wide):
            i, j = divmod(index, wide)
            tile = source[8 * i : 8 * i + 8, 128 * j : 128 * j + 128]
            out_ref[index // each, first_slot + index % each] = tile.astype(jnp.bfloat16)
        return first_slot + each

    slot = 0
    for ref in (gate_ref, up_ref, down_ref, first_ref, second_ref):
        slot = spread(ref, slot)
    slot = spread(x_rows, slot)
    spread(scaled, slot)


def pack(routes, route_gates, tokens, cotangent, gate_w, up_w, down_w, first, second, replica):
    count = lax.axis_size("expert")
    tok, width = tokens.shape
    half = first.shape[0]
    dests = 8
    steps = count // dests
    state_tiles = 5 * half * width // (count * 1024)
    tiles = state_tiles + 2 * capacity * width // 1024
    whole = lambda i, r: (0, 0)
    columns = lambda i, r: (i, r[0])
    own = lambda i, r: (i, 0)
    return pl.pallas_call(
        pack_kernel,
        out_shape=(
            jax.ShapeDtypeStruct((count, tiles, 8, 128), jnp.bfloat16),
            jax.ShapeDtypeStruct((count * capacity, tok), jnp.bfloat16),
        ),
        grid_spec=pltpu.PrefetchScalarGridSpec(
            num_scalar_prefetch=1,
            grid=(steps,),
            in_specs=[
                pl.BlockSpec(routes.shape, whole),
                pl.BlockSpec(route_gates.shape, whole),
                pl.BlockSpec(tokens.shape, whole),
                pl.BlockSpec(cotangent.shape, whole),
                pl.BlockSpec((width // steps, half), columns),
                pl.BlockSpec((width // steps, half), columns),
                pl.BlockSpec((half // steps, width), lambda i, r: (i + steps * r[0], 0)),
                pl.BlockSpec((half // steps, width), own),
                pl.BlockSpec((half // steps, width), own),
            ],
            out_specs=(
                pl.BlockSpec((dests, tiles, 8, 128), lambda i, r: (i, 0, 0, 0)),
                pl.BlockSpec((dests * capacity, tok), own),
            ),
            scratch_shapes=[pltpu.VMEM((count, tok), jnp.float32)] * 2,
        ),
        cost_estimate=pl.CostEstimate(
            flops=4 * count * capacity * tok * width, bytes_accessed=26_000_000, transcendentals=0
        ),
        name="pack",
    )(replica, routes, route_gates, tokens, cotangent, gate_w, up_w, down_w, first, second)


def forward_kernel(partner_ref, answer_ref, *refs):
    out_ref = refs[-1]
    out_tiles = answer_ref.shape[1]
    out_ref[:, :out_tiles] = answer_ref[...]
    for k, ref in enumerate(refs[:-1]):
        out_ref[k, out_tiles : out_tiles + ref.shape[1]] = ref[0]


def pack_onward(answer, gathered, partner, state_tiles, grad_tiles):
    count, out_tiles = answer.shape[:2]
    dests = 8

    def source(k):
        return pl.BlockSpec(
            (1, state_tiles, 8, 128), lambda i, p: (p[i * dests + k], 0, 0, 0)
        )

    tiles = out_tiles + state_tiles + grad_tiles
    return pl.pallas_call(
        forward_kernel,
        out_shape=jax.ShapeDtypeStruct((count, tiles, 8, 128), jnp.bfloat16),
        grid_spec=pltpu.PrefetchScalarGridSpec(
            num_scalar_prefetch=1,
            grid=(count // dests,),
            in_specs=[pl.BlockSpec((dests, out_tiles, 8, 128), lambda i, p: (i, 0, 0, 0))]
            + [source(k) for k in range(dests)],
            out_specs=pl.BlockSpec((dests, tiles, 8, 128), lambda i, p: (i, 0, 0, 0)),
        ),
        cost_estimate=pl.CostEstimate(flops=0, bytes_accessed=26_000_000, transcendentals=0),
        name="pack_onward",
    )(partner, answer, *([gathered] * dests))


def local(
    tokens,
    routes,
    route_gates,
    cotangent,
    swap_pairs,
    w_gate,
    w_up,
    w_down,
    moment_first,
    moment_second,
):
    count = lax.axis_size("expert")
    replica = lax.axis_index("dp")
    tok, width = tokens.shape
    gate_w, up_w, down_w = w_gate[0], w_up[0], w_down[0]
    half = gate_w.shape[1] // lax.axis_size("dp")
    share = half * width // (count * 1024)
    out_tiles = capacity * width // 1024

    packed, weigh = pack(
        routes.T,
        route_gates.T.astype(jnp.float32),
        tokens,
        cotangent,
        gate_w,
        up_w,
        down_w,
        moment_first[0],
        moment_second[0],
        replica.astype(jnp.int32).reshape(1),
    )
    spread = exchange(packed)
    spread, swap_pairs, weigh = lax.optimization_barrier((spread, swap_pairs, weigh))
    partner = partners(swap_pairs, count)

    state_tiles = 5 * share
    x_rows = from_tiles(
        spread[:, state_tiles : state_tiles + out_tiles], count * capacity, width
    )
    scaled = from_tiles(spread[:, state_tiles + out_tiles :], count * capacity, width)
    gate_pre = jnp.dot(x_rows, gate_w, preferred_element_type=jnp.float32)
    up_pre = jnp.dot(x_rows, up_w, preferred_element_type=jnp.float32)
    hidden = (jax.nn.silu(gate_pre) * up_pre).astype(jnp.bfloat16)
    partial = lax.dot_general(
        hidden, scaled, (((0,), (0,)), ((), ())), preferred_element_type=jnp.float32
    ).astype(jnp.bfloat16)
    pieces = to_tiles(partial, lax.axis_size("dp") * count)
    halves = lax.all_to_all(pieces, ("dp", "expert"), split_axis=0, concat_axis=0, tiled=True)

    outputs = jnp.dot(hidden, down_w, preferred_element_type=jnp.float32).astype(jnp.bfloat16)
    onward = pack_onward(to_tiles(outputs, count), spread, partner, state_tiles, share)
    onward, halves = lax.optimization_barrier((onward, halves))
    grad = jnp.sum(halves.reshape(-1, count, share, 8, 128).astype(jnp.float32), axis=0)
    grad = grad.astype(jnp.bfloat16)[partner]
    onward = lax.dynamic_update_slice(onward, grad, (0, out_tiles + state_tiles, 0, 0))
    landed = exchange(onward)

    returned = from_tiles(landed[:, :out_tiles], count * capacity, width)
    combined = lax.dot_general(
        weigh, returned, (((0,), (0,)), ((), ())), preferred_element_type=jnp.float32
    ).astype(jnp.bfloat16)
    gate_out, up_out, down_out, first_in, second_in, grad_in = [
        landed[:, out_tiles + i * share : out_tiles + (i + 1) * share] for i in range(6)
    ]
    first_out, second_out, step_out = [
        from_tiles(member, half, width)
        for member in adam_update(first_in, second_in, grad_in.astype(jnp.float32))
    ]
    return (
        combined,
        from_tiles(gate_out, width, half)[None],
        from_tiles(up_out, width, half)[None],
        from_tiles(down_out, half, width)[None],
        first_out[None],
        second_out[None],
        step_out[None],
    )


def solution(mesh):
    placed = (
        P(("dp", "expert"), None),
        P(("dp", "expert"), None),
        P(("dp", "expert"), None),
        P(("dp", "expert"), None),
        P(),
        P("expert", None, None),
        P("expert", None, None),
        P("expert", None, None),
        P("expert", "dp", None),
        P("expert", "dp", None),
    )
    return jax.shard_map(
        local,
        mesh=mesh,
        in_specs=placed,
        out_specs=(
            P(("dp", "expert"), None),
            P("expert", None, "dp"),
            P("expert", None, "dp"),
            P("expert", "dp", None),
            P("expert", "dp", None),
            P("expert", "dp", None),
            P("expert", "dp", None),
        ),
        check_vma=False,
    )
```

```python
import jax
import jax.numpy as jnp
from jax import lax
from jax.experimental import pallas as pl
from jax.experimental.pallas import tpu as pltpu
from jax.sharding import PartitionSpec as P

beta_first = 0.9
beta_second = 0.95
adam_eps = 1e-08
capacity = 16


def partners(swap_pairs, count):
    slot_ids = jnp.arange(count, dtype=jnp.int32)
    pair_left = swap_pairs[:, 0:1]
    pair_right = swap_pairs[:, 1:2]
    offsets = jnp.where(pair_left == slot_ids[None, :], pair_right - slot_ids[None, :], 0)
    offsets = offsets + jnp.where(pair_right == slot_ids[None, :], pair_left - slot_ids[None, :], 0)
    return slot_ids + jnp.sum(offsets, axis=0)


def to_tiles(array, pieces):
    rows, columns = array.shape
    tiles = array.reshape(rows // 8, 8, columns // 128, 128).transpose(0, 2, 1, 3)
    return tiles.reshape(pieces, -1, 8, 128)


def from_tiles(tiles, rows, columns):
    split = tiles.reshape(rows // 8, columns // 128, 8, 128).transpose(0, 2, 1, 3)
    return split.reshape(rows, columns)


def exchange(array):
    return lax.all_to_all(array, "expert", split_axis=0, concat_axis=0, tiled=True)


def adam_update(first_in, second_in, grad):
    first_moment = beta_first * first_in.astype(jnp.float32) + (1.0 - beta_first) * grad
    second_moment = beta_second * second_in.astype(jnp.float32) + (1.0 - beta_second) * grad * grad
    direction = first_moment / (jnp.sqrt(second_moment) + adam_eps)
    return (
        first_moment.astype(jnp.bfloat16),
        second_moment.astype(jnp.bfloat16),
        direction.astype(jnp.bfloat16),
    )


def pack_kernel(
    replica_ref,
    routes_ref,
    gates_ref,
    tokens_ref,
    cotangent_ref,
    gate_ref,
    up_ref,
    down_ref,
    first_ref,
    second_ref,
    out_ref,
    weigh_ref,
    stage_ref,
    rank_ref,
    weight_ref,
    in_sems,
    row_sems,
    state_sem,
):
    count, tok = rank_ref.shape
    tiles = stage_ref.shape[1]
    rows_tiles = capacity * tokens_ref.shape[1] // 1024
    state_tiles = tiles - 2 * rows_tiles
    steps = row_sems.shape[0]
    dests = count // steps
    replica = replica_ref[0]

    loads = []

    def load(source, slot, size):
        loads.append(
            pltpu.make_async_copy(
                source, stage_ref.at[:, slot : slot + size], in_sems.at[len(loads)]
            )
        )

    slot = 0
    for ref in (gate_ref, up_ref):
        tall, wide = ref.shape[1], ref.shape[2] // 2
        for a in range(tall):
            load(ref.at[:, a, pl.ds(replica * wide, wide)], slot, wide)
            slot += wide
    share = first_ref.shape[1]
    load(down_ref.at[pl.ds(replica * count, count)], slot, share)
    load(first_ref, slot + share, share)
    load(second_ref, slot + 2 * share, share)
    for copy in loads:
        copy.start()

    expert_ids = lax.broadcasted_iota(jnp.int32, (count, tok), 0)
    named = jnp.zeros((count, tok), jnp.float32)
    weight = jnp.zeros((count, tok), jnp.float32)
    gates = gates_ref[...].astype(jnp.float32)
    for k in range(routes_ref.shape[0]):
        hit = routes_ref[k : k + 1, :] == expert_ids
        named = jnp.where(hit, 1.0, named)
        weight = jnp.where(hit, gates[k : k + 1, :], weight)
    earlier = lax.broadcasted_iota(jnp.int32, (tok, tok), 0) < lax.broadcasted_iota(
        jnp.int32, (tok, tok), 1
    )
    rank_all = jnp.dot(
        named.astype(jnp.bfloat16),
        jnp.where(earlier, 1.0, 0.0).astype(jnp.bfloat16),
        preferred_element_type=jnp.float32,
    )
    rank_ref[...] = jnp.where(named > 0.0, rank_all, -1.0)
    weight_ref[...] = weight
    slot_ids = lax.broadcasted_iota(jnp.int32, (capacity, tok), 0).astype(jnp.float32)

    state_out = pltpu.make_async_copy(
        stage_ref.at[:, :state_tiles], out_ref.at[:, :state_tiles], state_sem
    )

    def rows_out(step):
        here = pl.ds(step * dests, dests)
        return pltpu.make_async_copy(
            stage_ref.at[here, state_tiles:], out_ref.at[here, state_tiles:], row_sems.at[step]
        )

    def one_step(step, carry):
        rank = rank_ref[pl.ds(pl.multiple_of(step * dests, dests), dests), :]
        weight = weight_ref[pl.ds(pl.multiple_of(step * dests, dests), dests), :]
        picks, weighs = [], []
        for s in range(dests):
            chosen = rank[s : s + 1, :] == slot_ids
            picks.append(jnp.where(chosen, 1.0, 0.0))
            weighs.append(jnp.where(chosen, weight[s : s + 1, :], 0.0))
        pick = jnp.concatenate(picks, axis=0).astype(jnp.bfloat16)
        weigh = jnp.concatenate(weighs, axis=0).astype(jnp.bfloat16)
        weigh_ref[pl.ds(pl.multiple_of(step * dests * capacity, 128), dests * capacity), :] = weigh
        for part, (lhs, rhs) in enumerate(((pick, tokens_ref), (weigh, cotangent_ref))):
            rows = jnp.dot(lhs, rhs[...], preferred_element_type=jnp.float32)
            wide = rows.shape[1] // 128
            for index in range(dests * rows_tiles):
                i, j = divmod(index, wide)
                stage_ref[
                    step * dests + index // rows_tiles,
                    state_tiles + part * rows_tiles + index % rows_tiles,
                ] = rows[8 * i : 8 * i + 8, 128 * j : 128 * j + 128].astype(jnp.bfloat16)
        rows_out(step).start()

        @pl.when(step == steps // 2)
        def _():
            for copy in loads:
                copy.wait()
            state_out.start()

        return carry

    lax.fori_loop(0, steps, one_step, 0)

    def one_wait(step, carry):
        rows_out(step).wait()
        return carry

    lax.fori_loop(0, steps, one_wait, 0)
    state_out.wait()


def pack(routes, route_gates, tokens, cotangent, gate_w, up_w, down_w, first, second, replica):
    count = lax.axis_size("expert")
    tok, width = tokens.shape
    share = first.size // (count * 1024)
    steps = 8
    tiles = 5 * share + 2 * capacity * width // 1024

    def columns(array):
        wide = array.shape[1] // 128
        return to_tiles(array, count).reshape(count, -1, wide, 8, 128)

    vmem = pl.BlockSpec(memory_space=pltpu.VMEM)
    anywhere = pl.BlockSpec(memory_space=pl.ANY)
    gate_view, up_view = columns(gate_w), columns(up_w)
    return pl.pallas_call(
        pack_kernel,
        out_shape=(
            jax.ShapeDtypeStruct((count, tiles, 8, 128), jnp.bfloat16),
            jax.ShapeDtypeStruct((count * capacity, tok), jnp.bfloat16),
        ),
        in_specs=[pl.BlockSpec(memory_space=pltpu.SMEM)] + [vmem] * 4 + [anywhere] * 5,
        out_specs=(anywhere, vmem),
        scratch_shapes=[
            pltpu.VMEM((count, tiles, 8, 128), jnp.bfloat16),
            pltpu.VMEM((count, tok), jnp.float32),
            pltpu.VMEM((count, tok), jnp.float32),
            pltpu.SemaphoreType.DMA((2 * gate_view.shape[1] + 3,)),
            pltpu.SemaphoreType.DMA((steps,)),
            pltpu.SemaphoreType.DMA,
        ],
        cost_estimate=pl.CostEstimate(
            flops=4 * count * capacity * tok * width, bytes_accessed=26_000_000, transcendentals=0
        ),
        name="pack",
    )(
        replica,
        routes,
        route_gates,
        tokens,
        cotangent,
        gate_view,
        up_view,
        to_tiles(down_w, 2 * count),
        to_tiles(first, count),
        to_tiles(second, count),
    )


def onward_kernel(partner_ref, answer_ref, state_ref, out_ref, stage_ref, state_sems, sems):
    count, out_tiles = answer_ref.shape[:2]
    tiles = stage_ref.shape[1]

    def piece(dest):
        return pltpu.make_async_copy(
            state_ref.at[partner_ref[dest]],
            stage_ref.at[dest, out_tiles:],
            state_sems.at[dest],
        )

    def start(dest, carry):
        piece(dest).start()
        return carry

    def wait(dest, carry):
        piece(dest).wait()
        return carry

    answer = pltpu.make_async_copy(answer_ref, stage_ref.at[:, :out_tiles], sems.at[0])
    answer.start()
    lax.fori_loop(0, count, start, 0)
    answer.wait()
    lax.fori_loop(0, count, wait, 0)
    leave = pltpu.make_async_copy(stage_ref, out_ref.at[:, :tiles], sems.at[1])
    leave.start()
    leave.wait()


def pack_onward(answer, gathered, partner, state_tiles, grad_tiles):
    count, out_tiles = answer.shape[:2]
    anywhere = pl.BlockSpec(memory_space=pl.ANY)
    return pl.pallas_call(
        onward_kernel,
        out_shape=jax.ShapeDtypeStruct(
            (count, out_tiles + state_tiles + grad_tiles, 8, 128), jnp.bfloat16
        ),
        in_specs=[pl.BlockSpec(memory_space=pltpu.SMEM), anywhere, anywhere],
        out_specs=anywhere,
        scratch_shapes=[
            pltpu.VMEM((count, out_tiles + state_tiles, 8, 128), jnp.bfloat16),
            pltpu.SemaphoreType.DMA((count,)),
            pltpu.SemaphoreType.DMA((2,)),
        ],
        cost_estimate=pl.CostEstimate(flops=0, bytes_accessed=24_000_000, transcendentals=0),
        name="pack_onward",
    )(partner, answer, gathered)


def grad_kernel(partner_ref, halves_ref, onward_ref, out_ref, stage_ref, sem):
    count, share = stage_ref.shape[:2]

    def one(dest, carry):
        place = partner_ref[dest]
        total = halves_ref[place].astype(jnp.float32)
        for r in range(1, halves_ref.shape[0] // count):
            total = total + halves_ref[r * count + place].astype(jnp.float32)
        stage_ref[dest] = total.astype(jnp.bfloat16)
        return carry

    lax.fori_loop(0, count, one, 0)
    leave = pltpu.make_async_copy(stage_ref, out_ref.at[:, out_ref.shape[1] - share :], sem)
    leave.start()
    leave.wait()


def add_grad(halves, onward, partner):
    count = onward.shape[0]
    share = halves.shape[1]
    anywhere = pl.BlockSpec(memory_space=pl.ANY)
    return pl.pallas_call(
        grad_kernel,
        out_shape=jax.ShapeDtypeStruct(onward.shape, onward.dtype),
        in_specs=[
            pl.BlockSpec(memory_space=pltpu.SMEM),
            pl.BlockSpec(memory_space=pltpu.VMEM),
            anywhere,
        ],
        out_specs=anywhere,
        scratch_shapes=[
            pltpu.VMEM((count, share, 8, 128), jnp.bfloat16),
            pltpu.SemaphoreType.DMA,
        ],
        input_output_aliases={2: 0},
        cost_estimate=pl.CostEstimate(flops=0, bytes_accessed=5_000_000, transcendentals=0),
        name="add_grad",
    )(partner, pltpu.with_memory_space_constraint(halves, pltpu.VMEM), onward)


def local(
    tokens,
    routes,
    route_gates,
    cotangent,
    swap_pairs,
    w_gate,
    w_up,
    w_down,
    moment_first,
    moment_second,
):
    count = lax.axis_size("expert")
    replica = lax.axis_index("dp")
    tok, width = tokens.shape
    gate_w, up_w, down_w = w_gate[0], w_up[0], w_down[0]
    half = gate_w.shape[1] // lax.axis_size("dp")
    share = half * width // (count * 1024)
    out_tiles = capacity * width // 1024

    packed, weigh = pack(
        routes.T,
        route_gates.T,
        tokens,
        cotangent,
        gate_w,
        up_w,
        down_w,
        moment_first[0],
        moment_second[0],
        replica.astype(jnp.int32).reshape(1),
    )
    spread = exchange(packed)
    spread, swap_pairs, weigh = lax.optimization_barrier((spread, swap_pairs, weigh))
    partner = partners(swap_pairs, count)

    state_tiles = 5 * share
    x_rows = from_tiles(
        spread[:, state_tiles : state_tiles + out_tiles], count * capacity, width
    )
    scaled = from_tiles(spread[:, state_tiles + out_tiles :], count * capacity, width)
    state, x_rows, scaled = lax.optimization_barrier((spread[:, :state_tiles], x_rows, scaled))
    gate_pre = jnp.dot(x_rows, gate_w, preferred_element_type=jnp.float32)
    up_pre = jnp.dot(x_rows, up_w, preferred_element_type=jnp.float32)
    hidden = (jax.nn.silu(gate_pre) * up_pre).astype(jnp.bfloat16)
    partial = lax.dot_general(
        hidden, scaled, (((0,), (0,)), ((), ())), preferred_element_type=jnp.float32
    ).astype(jnp.bfloat16)
    pieces = to_tiles(partial, lax.axis_size("dp") * count)
    halves = lax.all_to_all(pieces, ("dp", "expert"), split_axis=0, concat_axis=0, tiled=True)

    hidden, pieces = lax.optimization_barrier((hidden, pieces))
    outputs = jnp.dot(hidden, down_w, preferred_element_type=jnp.float32).astype(jnp.bfloat16)
    onward = pack_onward(to_tiles(outputs, count), state, partner, state_tiles, share)
    onward = add_grad(halves, onward, partner)
    landed = exchange(onward)

    returned = from_tiles(landed[:, :out_tiles], count * capacity, width)
    combined = lax.dot_general(
        weigh, returned, (((0,), (0,)), ((), ())), preferred_element_type=jnp.float32
    ).astype(jnp.bfloat16)
    gate_out, up_out, down_out, first_in, second_in, grad_in = [
        landed[:, out_tiles + i * share : out_tiles + (i + 1) * share] for i in range(6)
    ]
    first_out, second_out, step_out = [
        from_tiles(member, half, width)
        for member in adam_update(first_in, second_in, grad_in.astype(jnp.float32))
    ]
    return (
        combined,
        from_tiles(gate_out, width, half)[None],
        from_tiles(up_out, width, half)[None],
        from_tiles(down_out, half, width)[None],
        first_out[None],
        second_out[None],
        step_out[None],
    )


def solution(mesh):
    placed = (
        P(("dp", "expert"), None),
        P(("dp", "expert"), None),
        P(("dp", "expert"), None),
        P(("dp", "expert"), None),
        P(),
        P("expert", None, None),
        P("expert", None, None),
        P("expert", None, None),
        P("expert", "dp", None),
        P("expert", "dp", None),
    )
    return jax.shard_map(
        local,
        mesh=mesh,
        in_specs=placed,
        out_specs=(
            P(("dp", "expert"), None),
            P("expert", None, "dp"),
            P("expert", None, "dp"),
            P("expert", "dp", None),
            P("expert", "dp", None),
            P("expert", "dp", None),
            P("expert", "dp", None),
        ),
        check_vma=False,
    )
```

```python
import jax
import jax.numpy as jnp
from jax import lax
from jax.experimental import pallas as pl
from jax.experimental.pallas import tpu as pltpu
from jax.sharding import PartitionSpec as P

beta_first = 0.9
beta_second = 0.95
adam_eps = 1e-08
capacity = 16
vmem_limit = 24 * 1024 * 1024


def partners(swap_pairs, count):
    slot_ids = jnp.arange(count, dtype=jnp.int32)
    pair_left = swap_pairs[:, 0:1]
    pair_right = swap_pairs[:, 1:2]
    offsets = jnp.where(pair_left == slot_ids[None, :], pair_right - slot_ids[None, :], 0)
    offsets = offsets + jnp.where(pair_right == slot_ids[None, :], pair_left - slot_ids[None, :], 0)
    return slot_ids + jnp.sum(offsets, axis=0)


def to_tiles(array, pieces):
    rows, columns = array.shape
    tiles = array.reshape(rows // 8, 8, columns // 128, 128).transpose(0, 2, 1, 3)
    return tiles.reshape(pieces, -1, 8, 128)


def from_tiles(tiles, rows, columns):
    split = tiles.reshape(rows // 8, columns // 128, 8, 128).transpose(0, 2, 1, 3)
    return split.reshape(rows, columns)


def exchange(array):
    return lax.all_to_all(array, "expert", split_axis=0, concat_axis=0, tiled=True)


def adam_update(first_in, second_in, grad):
    first_moment = beta_first * first_in.astype(jnp.float32) + (1.0 - beta_first) * grad
    second_moment = beta_second * second_in.astype(jnp.float32) + (1.0 - beta_second) * grad * grad
    direction = first_moment / (jnp.sqrt(second_moment) + adam_eps)
    return (
        first_moment.astype(jnp.bfloat16),
        second_moment.astype(jnp.bfloat16),
        direction.astype(jnp.bfloat16),
    )


def pack_kernel(
    replica_ref,
    routes_hbm,
    gates_hbm,
    tokens_hbm,
    cotangent_hbm,
    gate_ref,
    up_ref,
    down_ref,
    first_ref,
    second_ref,
    out_ref,
    weigh_ref,
    routes_ref,
    gates_ref,
    tokens_ref,
    cotangent_ref,
    rank_ref,
    weight_ref,
    row_sems,
    in_sems,
):
    count, tok = rank_ref.shape
    rows_in = [
        pltpu.make_async_copy(source, target, row_sems.at[n])
        for n, (source, target) in enumerate(
            (
                (routes_hbm, routes_ref),
                (gates_hbm, gates_ref),
                (tokens_hbm, tokens_ref),
                (cotangent_hbm, cotangent_ref),
            )
        )
    ]
    for copy in rows_in:
        copy.start()
    rows_tiles = capacity * tokens_ref.shape[1] // 1024
    state_tiles = out_ref.shape[1] - 2 * rows_tiles
    dests = 8
    replica = replica_ref[0]

    loads = []

    def load(source, slot, size):
        loads.append(
            pltpu.make_async_copy(
                source, out_ref.at[:, slot : slot + size], in_sems.at[len(loads)]
            )
        )

    slot = 0
    for ref in (gate_ref, up_ref):
        tall, wide = ref.shape[1], ref.shape[2] // 2
        for a in range(tall):
            load(ref.at[:, a, pl.ds(replica * wide, wide)], slot, wide)
            slot += wide
    share = first_ref.shape[1]
    load(down_ref.at[pl.ds(replica * count, count)], slot, share)
    load(first_ref, slot + share, share)
    load(second_ref, slot + 2 * share, share)
    for copy in loads:
        copy.start()

    for copy in rows_in[:2]:
        copy.wait()
    expert_ids = lax.broadcasted_iota(jnp.int32, (count, tok), 0)
    named = jnp.zeros((count, tok), jnp.float32)
    weight = jnp.zeros((count, tok), jnp.float32)
    gates = gates_ref[...].astype(jnp.float32)
    for k in range(routes_ref.shape[0]):
        hit = routes_ref[k : k + 1, :] == expert_ids
        named = jnp.where(hit, 1.0, named)
        weight = jnp.where(hit, gates[k : k + 1, :], weight)
    earlier = lax.broadcasted_iota(jnp.int32, (tok, tok), 0) < lax.broadcasted_iota(
        jnp.int32, (tok, tok), 1
    )
    rank_all = jnp.dot(
        named.astype(jnp.bfloat16),
        jnp.where(earlier, 1.0, 0.0).astype(jnp.bfloat16),
        preferred_element_type=jnp.float32,
    )
    rank_ref[...] = jnp.where(named > 0.0, rank_all, -1.0)
    weight_ref[...] = weight
    slot_ids = lax.broadcasted_iota(jnp.int32, (capacity, tok), 0).astype(jnp.float32)
    for copy in rows_in[2:]:
        copy.wait()

    def one_step(step, carry):
        rank = rank_ref[pl.ds(pl.multiple_of(step * dests, dests), dests), :]
        weight = weight_ref[pl.ds(pl.multiple_of(step * dests, dests), dests), :]
        picks, weighs = [], []
        for s in range(dests):
            chosen = rank[s : s + 1, :] == slot_ids
            picks.append(jnp.where(chosen, 1.0, 0.0))
            weighs.append(jnp.where(chosen, weight[s : s + 1, :], 0.0))
        pick = jnp.concatenate(picks, axis=0).astype(jnp.bfloat16)
        weigh = jnp.concatenate(weighs, axis=0).astype(jnp.bfloat16)
        weigh_ref[pl.ds(pl.multiple_of(step * dests * capacity, 128), dests * capacity), :] = weigh
        for part, (lhs, rhs) in enumerate(((pick, tokens_ref), (weigh, cotangent_ref))):
            rows = jnp.dot(lhs, rhs[...], preferred_element_type=jnp.float32)
            wide = rows.shape[1] // 128
            for index in range(dests * rows_tiles):
                i, j = divmod(index, wide)
                out_ref[
                    step * dests + index // rows_tiles,
                    state_tiles + part * rows_tiles + index % rows_tiles,
                ] = rows[8 * i : 8 * i + 8, 128 * j : 128 * j + 128].astype(jnp.bfloat16)
        return carry

    lax.fori_loop(0, count // dests, one_step, 0)
    for copy in loads:
        copy.wait()


def pack(routes, route_gates, tokens, cotangent, gate_w, up_w, down_w, first, second, replica):
    count = lax.axis_size("expert")
    tok, width = tokens.shape
    share = first.size // (count * 1024)
    tiles = 5 * share + 2 * capacity * width // 1024

    def columns(array):
        wide = array.shape[1] // 128
        return to_tiles(array, count).reshape(count, -1, wide, 8, 128)

    vmem = pl.BlockSpec(memory_space=pltpu.VMEM)
    anywhere = pl.BlockSpec(memory_space=pl.ANY)
    gate_view, up_view = columns(gate_w), columns(up_w)
    return pl.pallas_call(
        pack_kernel,
        out_shape=(
            pltpu.VMEM((count, tiles, 8, 128), jnp.bfloat16),
            jax.ShapeDtypeStruct((count * capacity, tok), jnp.bfloat16),
        ),
        in_specs=[pl.BlockSpec(memory_space=pltpu.SMEM)] + [anywhere] * 9,
        out_specs=(vmem, vmem),
        scratch_shapes=[
            pltpu.VMEM(routes.shape, routes.dtype),
            pltpu.VMEM(route_gates.shape, route_gates.dtype),
            pltpu.VMEM(tokens.shape, tokens.dtype),
            pltpu.VMEM(cotangent.shape, cotangent.dtype),
            pltpu.VMEM((count, tok), jnp.float32),
            pltpu.VMEM((count, tok), jnp.float32),
            pltpu.SemaphoreType.DMA((4,)),
            pltpu.SemaphoreType.DMA((2 * gate_view.shape[1] + 3,)),
        ],
        cost_estimate=pl.CostEstimate(
            flops=4 * count * capacity * tok * width, bytes_accessed=26_000_000, transcendentals=0
        ),
        compiler_params=pltpu.CompilerParams(vmem_limit_bytes=vmem_limit),
        name="pack",
    )(
        replica,
        *[
            pltpu.with_memory_space_constraint(member, pltpu.HBM)
            for member in (
                routes,
                route_gates,
                tokens,
                cotangent,
                gate_view,
                up_view,
                to_tiles(down_w, 2 * count),
                to_tiles(first, count),
                to_tiles(second, count),
            )
        ],
    )


def rows_kernel(landed_ref, x_ref, scaled_ref, sems):
    out_tiles = x_ref.shape[1]
    state_tiles = landed_ref.shape[1] - 2 * out_tiles
    copies = [
        pltpu.make_async_copy(
            landed_ref.at[:, state_tiles + n * out_tiles : state_tiles + (n + 1) * out_tiles],
            target,
            sems.at[n],
        )
        for n, target in enumerate((x_ref, scaled_ref))
    ]
    for copy in copies:
        copy.start()
    for copy in copies:
        copy.wait()


def take_rows(landed, out_tiles):
    count = landed.shape[0]
    vmem = pl.BlockSpec(memory_space=pltpu.VMEM)
    rows = pltpu.VMEM((count, out_tiles, 8, 128), jnp.bfloat16)
    return pl.pallas_call(
        rows_kernel,
        out_shape=(rows, rows),
        in_specs=[pl.BlockSpec(memory_space=pl.ANY)],
        out_specs=(vmem, vmem),
        scratch_shapes=[pltpu.SemaphoreType.DMA((2,))],
        compiler_params=pltpu.CompilerParams(vmem_limit_bytes=vmem_limit),
        cost_estimate=pl.CostEstimate(flops=0, bytes_accessed=8_400_000, transcendentals=0),
        name="take_rows",
    )(pltpu.with_memory_space_constraint(landed, pltpu.HBM))


def onward_kernel(partner_ref, answer_ref, state_ref, out_ref, stage_ref, state_sems, sems):
    count, out_tiles = answer_ref.shape[:2]
    tiles = stage_ref.shape[1]

    def piece(dest):
        return pltpu.make_async_copy(
            state_ref.at[partner_ref[dest], : tiles - out_tiles],
            stage_ref.at[dest, out_tiles:],
            state_sems.at[dest],
        )

    def start(dest, carry):
        piece(dest).start()
        return carry

    def wait(dest, carry):
        piece(dest).wait()
        return carry

    answer = pltpu.make_async_copy(answer_ref, stage_ref.at[:, :out_tiles], sems.at[0])
    answer.start()
    lax.fori_loop(0, count, start, 0)
    answer.wait()
    lax.fori_loop(0, count, wait, 0)
    leave = pltpu.make_async_copy(stage_ref, out_ref.at[:, :tiles], sems.at[1])
    leave.start()
    leave.wait()


def pack_onward(answer, gathered, partner, state_tiles, grad_tiles):
    count, out_tiles = answer.shape[:2]
    anywhere = pl.BlockSpec(memory_space=pl.ANY)
    return pl.pallas_call(
        onward_kernel,
        out_shape=jax.ShapeDtypeStruct(
            (count, out_tiles + state_tiles + grad_tiles, 8, 128), jnp.bfloat16
        ),
        in_specs=[pl.BlockSpec(memory_space=pltpu.SMEM), anywhere, anywhere],
        out_specs=anywhere,
        scratch_shapes=[
            pltpu.VMEM((count, out_tiles + state_tiles, 8, 128), jnp.bfloat16),
            pltpu.SemaphoreType.DMA((count,)),
            pltpu.SemaphoreType.DMA((2,)),
        ],
        cost_estimate=pl.CostEstimate(flops=0, bytes_accessed=24_000_000, transcendentals=0),
        name="pack_onward",
    )(partner, answer, pltpu.with_memory_space_constraint(gathered, pltpu.HBM))


def grad_kernel(partner_ref, halves_ref, onward_ref, out_ref, stage_ref, sem):
    count, share = stage_ref.shape[:2]

    def one(dest, carry):
        place = partner_ref[dest]
        total = halves_ref[place].astype(jnp.float32)
        for r in range(1, halves_ref.shape[0] // count):
            total = total + halves_ref[r * count + place].astype(jnp.float32)
        stage_ref[dest] = total.astype(jnp.bfloat16)
        return carry

    lax.fori_loop(0, count, one, 0)
    leave = pltpu.make_async_copy(stage_ref, out_ref.at[:, out_ref.shape[1] - share :], sem)
    leave.start()
    leave.wait()


def add_grad(halves, onward, partner):
    count = onward.shape[0]
    share = halves.shape[1]
    anywhere = pl.BlockSpec(memory_space=pl.ANY)
    return pl.pallas_call(
        grad_kernel,
        out_shape=jax.ShapeDtypeStruct(onward.shape, onward.dtype),
        in_specs=[
            pl.BlockSpec(memory_space=pltpu.SMEM),
            pl.BlockSpec(memory_space=pltpu.VMEM),
            anywhere,
        ],
        out_specs=anywhere,
        scratch_shapes=[
            pltpu.VMEM((count, share, 8, 128), jnp.bfloat16),
            pltpu.SemaphoreType.DMA,
        ],
        input_output_aliases={2: 0},
        cost_estimate=pl.CostEstimate(flops=0, bytes_accessed=5_000_000, transcendentals=0),
        name="add_grad",
    )(partner, pltpu.with_memory_space_constraint(halves, pltpu.VMEM), onward)


def local(
    tokens,
    routes,
    route_gates,
    cotangent,
    swap_pairs,
    w_gate,
    w_up,
    w_down,
    moment_first,
    moment_second,
):
    count = lax.axis_size("expert")
    replica = lax.axis_index("dp")
    tok, width = tokens.shape
    gate_w, up_w, down_w = w_gate[0], w_up[0], w_down[0]
    half = gate_w.shape[1] // lax.axis_size("dp")
    share = half * width // (count * 1024)
    out_tiles = capacity * width // 1024

    packed, weigh = pack(
        routes.T,
        route_gates.T,
        tokens,
        cotangent,
        gate_w,
        up_w,
        down_w,
        moment_first[0],
        moment_second[0],
        replica.astype(jnp.int32).reshape(1),
    )
    spread = exchange(packed)
    spread, swap_pairs, weigh = lax.optimization_barrier((spread, swap_pairs, weigh))
    partner = partners(swap_pairs, count)

    state_tiles = 5 * share
    x_tiles, scaled_tiles = take_rows(spread, out_tiles)
    x_rows = from_tiles(x_tiles, count * capacity, width)
    scaled = from_tiles(scaled_tiles, count * capacity, width)
    gate_pre = jnp.dot(x_rows, gate_w, preferred_element_type=jnp.float32)
    up_pre = jnp.dot(x_rows, up_w, preferred_element_type=jnp.float32)
    hidden = (jax.nn.silu(gate_pre) * up_pre).astype(jnp.bfloat16)
    partial = lax.dot_general(
        hidden, scaled, (((0,), (0,)), ((), ())), preferred_element_type=jnp.float32
    ).astype(jnp.bfloat16)
    pieces = to_tiles(partial, lax.axis_size("dp") * count)
    halves = lax.all_to_all(pieces, ("dp", "expert"), split_axis=0, concat_axis=0, tiled=True)

    hidden, pieces = lax.optimization_barrier((hidden, pieces))
    outputs = jnp.dot(hidden, down_w, preferred_element_type=jnp.float32).astype(jnp.bfloat16)
    onward = pack_onward(to_tiles(outputs, count), spread, partner, state_tiles, share)
    onward = add_grad(halves, onward, partner)
    landed = exchange(onward)

    returned = from_tiles(landed[:, :out_tiles], count * capacity, width)
    combined = lax.dot_general(
        weigh, returned, (((0,), (0,)), ((), ())), preferred_element_type=jnp.float32
    ).astype(jnp.bfloat16)
    gate_out, up_out, down_out, first_in, second_in, grad_in = [
        landed[:, out_tiles + i * share : out_tiles + (i + 1) * share] for i in range(6)
    ]
    first_out, second_out, step_out = [
        from_tiles(member, half, width)
        for member in adam_update(first_in, second_in, grad_in.astype(jnp.float32))
    ]
    return (
        combined,
        from_tiles(gate_out, width, half)[None],
        from_tiles(up_out, width, half)[None],
        from_tiles(down_out, half, width)[None],
        first_out[None],
        second_out[None],
        step_out[None],
    )


def solution(mesh):
    placed = (
        P(("dp", "expert"), None),
        P(("dp", "expert"), None),
        P(("dp", "expert"), None),
        P(("dp", "expert"), None),
        P(),
        P("expert", None, None),
        P("expert", None, None),
        P("expert", None, None),
        P("expert", "dp", None),
        P("expert", "dp", None),
    )
    return jax.shard_map(
        local,
        mesh=mesh,
        in_specs=placed,
        out_specs=(
            P(("dp", "expert"), None),
            P("expert", None, "dp"),
            P("expert", None, "dp"),
            P("expert", "dp", None),
            P("expert", "dp", None),
            P("expert", "dp", None),
            P("expert", "dp", None),
        ),
        check_vma=False,
    )
```

```python
import jax
import jax.numpy as jnp
from jax import lax
from jax.experimental import pallas as pl
from jax.experimental.pallas import tpu as pltpu
from jax.sharding import PartitionSpec as P

beta_first = 0.9
beta_second = 0.95
adam_eps = 1e-08
capacity = 16
vmem_limit = 24 * 1024 * 1024


def partners(swap_pairs, count):
    slot_ids = jnp.arange(count, dtype=jnp.int32)
    pair_left = swap_pairs[:, 0:1]
    pair_right = swap_pairs[:, 1:2]
    offsets = jnp.where(pair_left == slot_ids[None, :], pair_right - slot_ids[None, :], 0)
    offsets = offsets + jnp.where(pair_right == slot_ids[None, :], pair_left - slot_ids[None, :], 0)
    return slot_ids + jnp.sum(offsets, axis=0)


def to_tiles(array, pieces):
    rows, columns = array.shape
    tiles = array.reshape(rows // 8, 8, columns // 128, 128).transpose(0, 2, 1, 3)
    return tiles.reshape(pieces, -1, 8, 128)


def from_tiles(tiles, rows, columns):
    split = tiles.reshape(rows // 8, columns // 128, 8, 128).transpose(0, 2, 1, 3)
    return split.reshape(rows, columns)


def exchange(array):
    return lax.all_to_all(array, "expert", split_axis=0, concat_axis=0, tiled=True)


def adam_update(first_in, second_in, grad):
    first_moment = beta_first * first_in.astype(jnp.float32) + (1.0 - beta_first) * grad
    second_moment = beta_second * second_in.astype(jnp.float32) + (1.0 - beta_second) * grad * grad
    direction = first_moment / (jnp.sqrt(second_moment) + adam_eps)
    return (
        first_moment.astype(jnp.bfloat16),
        second_moment.astype(jnp.bfloat16),
        direction.astype(jnp.bfloat16),
    )


def pack_kernel(
    replica_ref,
    routes_hbm,
    gates_hbm,
    tokens_hbm,
    cotangent_hbm,
    gate_ref,
    up_ref,
    down_ref,
    first_ref,
    second_ref,
    out_ref,
    weigh_ref,
    routes_ref,
    gates_ref,
    tokens_ref,
    cotangent_ref,
    rank_ref,
    weight_ref,
    row_sems,
    in_sems,
):
    count, tok = rank_ref.shape
    rows_in = [
        pltpu.make_async_copy(source, target, row_sems.at[n])
        for n, (source, target) in enumerate(
            (
                (routes_hbm, routes_ref),
                (gates_hbm, gates_ref),
                (tokens_hbm, tokens_ref),
                (cotangent_hbm, cotangent_ref),
            )
        )
    ]
    for copy in rows_in:
        copy.start()
    rows_tiles = capacity * tokens_ref.shape[1] // 1024
    state_tiles = out_ref.shape[1] - 2 * rows_tiles
    dests = 32
    replica = replica_ref[0]

    loads = []

    def load(source, slot, size):
        loads.append(
            pltpu.make_async_copy(
                source, out_ref.at[:, slot : slot + size], in_sems.at[len(loads)]
            )
        )

    slot = 0
    for ref in (gate_ref, up_ref):
        tall, wide = ref.shape[1], ref.shape[2] // 2
        for a in range(tall):
            load(ref.at[:, a, pl.ds(replica * wide, wide)], slot, wide)
            slot += wide
    share = first_ref.shape[1]
    load(down_ref.at[pl.ds(replica * count, count)], slot, share)
    load(first_ref, slot + share, share)
    load(second_ref, slot + 2 * share, share)
    for copy in loads:
        copy.start()

    for copy in rows_in[:2]:
        copy.wait()
    expert_ids = lax.broadcasted_iota(jnp.int32, (count, tok), 0)
    named = jnp.zeros((count, tok), jnp.float32)
    weight = jnp.zeros((count, tok), jnp.float32)
    gates = gates_ref[...].astype(jnp.float32)
    for k in range(routes_ref.shape[0]):
        hit = routes_ref[k : k + 1, :] == expert_ids
        named = jnp.where(hit, 1.0, named)
        weight = jnp.where(hit, gates[k : k + 1, :], weight)
    earlier = lax.broadcasted_iota(jnp.int32, (tok, tok), 0) < lax.broadcasted_iota(
        jnp.int32, (tok, tok), 1
    )
    rank_all = jnp.dot(
        named.astype(jnp.bfloat16),
        jnp.where(earlier, 1.0, 0.0).astype(jnp.bfloat16),
        preferred_element_type=jnp.float32,
    )
    rank_ref[...] = jnp.where(named > 0.0, rank_all, -1.0)
    weight_ref[...] = weight
    slot_ids = lax.broadcasted_iota(jnp.int32, (capacity, tok), 0).astype(jnp.float32)
    for copy in rows_in[2:]:
        copy.wait()

    def one_step(step, carry):
        rank = rank_ref[pl.ds(pl.multiple_of(step * dests, dests), dests), :]
        weight = weight_ref[pl.ds(pl.multiple_of(step * dests, dests), dests), :]
        picks, weighs = [], []
        for s in range(dests):
            chosen = rank[s : s + 1, :] == slot_ids
            picks.append(jnp.where(chosen, 1.0, 0.0))
            weighs.append(jnp.where(chosen, weight[s : s + 1, :], 0.0))
        pick = jnp.concatenate(picks, axis=0).astype(jnp.bfloat16)
        weigh = jnp.concatenate(weighs, axis=0).astype(jnp.bfloat16)
        weigh_ref[pl.ds(pl.multiple_of(step * dests * capacity, 128), dests * capacity), :] = weigh
        for part, (lhs, rhs) in enumerate(((pick, tokens_ref), (weigh, cotangent_ref))):
            rows = jnp.dot(lhs, rhs[...], preferred_element_type=jnp.float32)
            wide = rows.shape[1] // 128
            for index in range(dests * rows_tiles):
                i, j = divmod(index, wide)
                out_ref[
                    step * dests + index // rows_tiles,
                    state_tiles + part * rows_tiles + index % rows_tiles,
                ] = rows[8 * i : 8 * i + 8, 128 * j : 128 * j + 128].astype(jnp.bfloat16)
        return carry

    lax.fori_loop(0, count // dests, one_step, 0)
    for copy in loads:
        copy.wait()


def pack(routes, route_gates, tokens, cotangent, gate_w, up_w, down_w, first, second, replica):
    count = lax.axis_size("expert")
    tok, width = tokens.shape
    share = first.size // (count * 1024)
    tiles = 5 * share + 2 * capacity * width // 1024

    def columns(array):
        wide = array.shape[1] // 128
        return to_tiles(array, count).reshape(count, -1, wide, 8, 128)

    vmem = pl.BlockSpec(memory_space=pltpu.VMEM)
    anywhere = pl.BlockSpec(memory_space=pl.ANY)
    gate_view, up_view = columns(gate_w), columns(up_w)
    return pl.pallas_call(
        pack_kernel,
        out_shape=(
            pltpu.VMEM((count, tiles, 8, 128), jnp.bfloat16),
            jax.ShapeDtypeStruct((count * capacity, tok), jnp.bfloat16),
        ),
        in_specs=[pl.BlockSpec(memory_space=pltpu.SMEM)] + [anywhere] * 9,
        out_specs=(vmem, vmem),
        scratch_shapes=[
            pltpu.VMEM(routes.shape, routes.dtype),
            pltpu.VMEM(route_gates.shape, route_gates.dtype),
            pltpu.VMEM(tokens.shape, tokens.dtype),
            pltpu.VMEM(cotangent.shape, cotangent.dtype),
            pltpu.VMEM((count, tok), jnp.float32),
            pltpu.VMEM((count, tok), jnp.float32),
            pltpu.SemaphoreType.DMA((4,)),
            pltpu.SemaphoreType.DMA((2 * gate_view.shape[1] + 3,)),
        ],
        cost_estimate=pl.CostEstimate(
            flops=4 * count * capacity * tok * width, bytes_accessed=26_000_000, transcendentals=0
        ),
        compiler_params=pltpu.CompilerParams(vmem_limit_bytes=vmem_limit),
        name="pack",
    )(
        replica,
        *[
            pltpu.with_memory_space_constraint(member, pltpu.HBM)
            for member in (
                routes,
                route_gates,
                tokens,
                cotangent,
                gate_view,
                up_view,
                to_tiles(down_w, 2 * count),
                to_tiles(first, count),
                to_tiles(second, count),
            )
        ],
    )


def rows_kernel(landed_ref, x_ref, scaled_ref, sems):
    out_tiles = x_ref.shape[1]
    state_tiles = landed_ref.shape[1] - 2 * out_tiles
    parts = sems.shape[1]
    each = x_ref.shape[0] // parts
    copies = [
        pltpu.make_async_copy(
            landed_ref.at[
                part * each : (part + 1) * each,
                state_tiles + n * out_tiles : state_tiles + (n + 1) * out_tiles,
            ],
            target.at[part * each : (part + 1) * each],
            sems.at[n, part],
        )
        for n, target in enumerate((x_ref, scaled_ref))
        for part in range(parts)
    ]
    for copy in copies:
        copy.start()
    for copy in copies:
        copy.wait()


def take_rows(landed, out_tiles):
    count = landed.shape[0]
    vmem = pl.BlockSpec(memory_space=pltpu.VMEM)
    rows = pltpu.VMEM((count, out_tiles, 8, 128), jnp.bfloat16)
    return pl.pallas_call(
        rows_kernel,
        out_shape=(rows, rows),
        in_specs=[pl.BlockSpec(memory_space=pl.ANY)],
        out_specs=(vmem, vmem),
        scratch_shapes=[pltpu.SemaphoreType.DMA((2, 8))],
        compiler_params=pltpu.CompilerParams(vmem_limit_bytes=vmem_limit),
        cost_estimate=pl.CostEstimate(flops=0, bytes_accessed=8_400_000, transcendentals=0),
        name="take_rows",
    )(pltpu.with_memory_space_constraint(landed, pltpu.HBM))


def onward_kernel(partner_ref, answer_ref, state_ref, out_ref, stage_ref, state_sems, sems):
    count, out_tiles = answer_ref.shape[:2]
    tiles = stage_ref.shape[1]

    def piece(dest):
        return pltpu.make_async_copy(
            state_ref.at[partner_ref[dest], : tiles - out_tiles],
            stage_ref.at[dest, out_tiles:],
            state_sems.at[dest],
        )

    def start(dest, carry):
        piece(dest).start()
        return carry

    def wait(dest, carry):
        piece(dest).wait()
        return carry

    answer = pltpu.make_async_copy(answer_ref, stage_ref.at[:, :out_tiles], sems.at[0])
    answer.start()
    lax.fori_loop(0, count, start, 0)
    answer.wait()
    lax.fori_loop(0, count, wait, 0)
    leave = pltpu.make_async_copy(stage_ref, out_ref.at[:, :tiles], sems.at[1])
    leave.start()
    leave.wait()


def pack_onward(answer, gathered, partner, state_tiles, grad_tiles):
    count, out_tiles = answer.shape[:2]
    anywhere = pl.BlockSpec(memory_space=pl.ANY)
    return pl.pallas_call(
        onward_kernel,
        out_shape=jax.ShapeDtypeStruct(
            (count, out_tiles + state_tiles + grad_tiles, 8, 128), jnp.bfloat16
        ),
        in_specs=[pl.BlockSpec(memory_space=pltpu.SMEM), anywhere, anywhere],
        out_specs=anywhere,
        scratch_shapes=[
            pltpu.VMEM((count, out_tiles + state_tiles, 8, 128), jnp.bfloat16),
            pltpu.SemaphoreType.DMA((count,)),
            pltpu.SemaphoreType.DMA((2,)),
        ],
        cost_estimate=pl.CostEstimate(flops=0, bytes_accessed=24_000_000, transcendentals=0),
        name="pack_onward",
    )(partner, answer, pltpu.with_memory_space_constraint(gathered, pltpu.HBM))


def grad_kernel(partner_ref, halves_ref, onward_ref, out_ref, stage_ref, sems):
    count, share = stage_ref.shape[:2]
    chunks = sems.shape[0]
    each = count // chunks

    def one(dest, carry):
        place = partner_ref[dest]
        total = halves_ref[place].astype(jnp.float32)
        for r in range(1, halves_ref.shape[0] // count):
            total = total + halves_ref[r * count + place].astype(jnp.float32)
        stage_ref[dest] = total.astype(jnp.bfloat16)
        return carry

    leaves = []
    for chunk in range(chunks):
        here = slice(chunk * each, (chunk + 1) * each)
        lax.fori_loop(chunk * each, (chunk + 1) * each, one, 0, unroll=4)
        leaves.append(
            pltpu.make_async_copy(
                stage_ref.at[here], out_ref.at[here, out_ref.shape[1] - share :], sems.at[chunk]
            )
        )
        leaves[-1].start()
    for leave in leaves:
        leave.wait()


def add_grad(halves, onward, partner):
    count = onward.shape[0]
    share = halves.shape[1]
    anywhere = pl.BlockSpec(memory_space=pl.ANY)
    return pl.pallas_call(
        grad_kernel,
        out_shape=jax.ShapeDtypeStruct(onward.shape, onward.dtype),
        in_specs=[
            pl.BlockSpec(memory_space=pltpu.SMEM),
            pl.BlockSpec(memory_space=pltpu.VMEM),
            anywhere,
        ],
        out_specs=anywhere,
        scratch_shapes=[
            pltpu.VMEM((count, share, 8, 128), jnp.bfloat16),
            pltpu.SemaphoreType.DMA((4,)),
        ],
        input_output_aliases={2: 0},
        cost_estimate=pl.CostEstimate(flops=0, bytes_accessed=5_000_000, transcendentals=0),
        name="add_grad",
    )(partner, pltpu.with_memory_space_constraint(halves, pltpu.VMEM), onward)


def update_kernel(
    landed_ref,
    gate_ref,
    up_ref,
    down_ref,
    first_ref,
    second_ref,
    step_ref,
    stage_ref,
    weight_sems,
    state_sems,
):
    count, share = gate_ref.shape[:2]
    slot = landed_ref.shape[1] - 6 * share
    chunks = state_sems.shape[1]
    each = count // chunks
    weights = [
        pltpu.make_async_copy(
            landed_ref.at[:, slot + n * share : slot + (n + 1) * share], target, weight_sems.at[n]
        )
        for n, target in enumerate((gate_ref, up_ref, down_ref))
    ]
    for copy in weights:
        copy.start()

    def leave(n, chunk):
        here = pl.ds(chunk * each, each)
        target = (first_ref, second_ref, step_ref)[n]
        return pltpu.make_async_copy(
            stage_ref.at[n, here], target.at[here], state_sems.at[n, chunk]
        )

    def one_piece(piece, carry):
        first_in, second_in, grad = [
            landed_ref[piece, slot + n * share : slot + (n + 1) * share] for n in (3, 4, 5)
        ]
        for n, member in enumerate(adam_update(first_in, second_in, grad.astype(jnp.float32))):
            stage_ref[n, piece] = member
        return carry

    def two_pieces(chunk):
        def both(pair, carry):
            one_piece(chunk * each + 2 * pair, carry)
            return one_piece(chunk * each + 2 * pair + 1, carry)

        return both

    def one_chunk(chunk, carry):
        lax.fori_loop(0, each // 2, two_pieces(chunk), 0)
        for n in range(3):
            leave(n, chunk).start()
        return carry

    def one_wait(chunk, carry):
        for n in range(3):
            leave(n, chunk).wait()
        return carry

    lax.fori_loop(0, chunks, one_chunk, 0)
    lax.fori_loop(0, chunks, one_wait, 0)
    for copy in weights:
        copy.wait()


def update(landed, share):
    count = landed.shape[0]
    anywhere = pl.BlockSpec(memory_space=pl.ANY)
    piece = jax.ShapeDtypeStruct((count, share, 8, 128), jnp.bfloat16)
    return pl.pallas_call(
        update_kernel,
        out_shape=(piece,) * 6,
        in_specs=[pl.BlockSpec(memory_space=pltpu.VMEM)],
        out_specs=(anywhere,) * 6,
        scratch_shapes=[
            pltpu.VMEM((3, count, share, 8, 128), jnp.bfloat16),
            pltpu.SemaphoreType.DMA((3,)),
            pltpu.SemaphoreType.DMA((3, 8)),
        ],
        compiler_params=pltpu.CompilerParams(vmem_limit_bytes=vmem_limit),
        cost_estimate=pl.CostEstimate(
            flops=20_000_000, bytes_accessed=9_500_000, transcendentals=1_600_000
        ),
        name="update",
    )(pltpu.with_memory_space_constraint(landed, pltpu.VMEM))


def local(
    tokens,
    routes,
    route_gates,
    cotangent,
    swap_pairs,
    w_gate,
    w_up,
    w_down,
    moment_first,
    moment_second,
):
    count = lax.axis_size("expert")
    replica = lax.axis_index("dp")
    tok, width = tokens.shape
    gate_w, up_w, down_w = w_gate[0], w_up[0], w_down[0]
    half = gate_w.shape[1] // lax.axis_size("dp")
    share = half * width // (count * 1024)
    out_tiles = capacity * width // 1024

    packed, weigh = pack(
        routes.T,
        route_gates.T,
        tokens,
        cotangent,
        gate_w,
        up_w,
        down_w,
        moment_first[0],
        moment_second[0],
        replica.astype(jnp.int32).reshape(1),
    )
    spread = exchange(packed)
    spread, swap_pairs, weigh = lax.optimization_barrier((spread, swap_pairs, weigh))
    partner = partners(swap_pairs, count)

    state_tiles = 5 * share
    x_tiles, scaled_tiles = take_rows(spread, out_tiles)
    x_rows = from_tiles(x_tiles, count * capacity, width)
    scaled = from_tiles(scaled_tiles, count * capacity, width)
    gate_pre = jnp.dot(x_rows, gate_w, preferred_element_type=jnp.float32)
    up_pre = jnp.dot(x_rows, up_w, preferred_element_type=jnp.float32)
    hidden = (jax.nn.silu(gate_pre) * up_pre).astype(jnp.bfloat16)
    partial = lax.dot_general(
        hidden, scaled, (((0,), (0,)), ((), ())), preferred_element_type=jnp.float32
    ).astype(jnp.bfloat16)
    pieces = to_tiles(partial, lax.axis_size("dp") * count)
    halves = lax.all_to_all(pieces, ("dp", "expert"), split_axis=0, concat_axis=0, tiled=True)

    hidden, pieces = lax.optimization_barrier((hidden, pieces))
    outputs = jnp.dot(hidden, down_w, preferred_element_type=jnp.float32).astype(jnp.bfloat16)
    onward = pack_onward(to_tiles(outputs, count), spread, partner, state_tiles, share)
    onward = add_grad(halves, onward, partner)
    landed = exchange(onward)

    returned = from_tiles(landed[:, :out_tiles], count * capacity, width)
    combined = lax.dot_general(
        weigh, returned, (((0,), (0,)), ((), ())), preferred_element_type=jnp.float32
    ).astype(jnp.bfloat16)
    gate_out, up_out, down_out, first_out, second_out, step_out = update(landed, share)
    return (
        combined,
        from_tiles(gate_out, width, half)[None],
        from_tiles(up_out, width, half)[None],
        from_tiles(down_out, half, width)[None],
        from_tiles(first_out, half, width)[None],
        from_tiles(second_out, half, width)[None],
        from_tiles(step_out, half, width)[None],
    )


def solution(mesh):
    placed = (
        P(("dp", "expert"), None),
        P(("dp", "expert"), None),
        P(("dp", "expert"), None),
        P(("dp", "expert"), None),
        P(),
        P("expert", None, None),
        P("expert", None, None),
        P("expert", None, None),
        P("expert", "dp", None),
        P("expert", "dp", None),
    )
    return jax.shard_map(
        local,
        mesh=mesh,
        in_specs=placed,
        out_specs=(
            P(("dp", "expert"), None),
            P("expert", None, "dp"),
            P("expert", None, "dp"),
            P("expert", "dp", None),
            P("expert", "dp", None),
            P("expert", "dp", None),
            P("expert", "dp", None),
        ),
        check_vma=False,
    )
```

```python
import jax
import jax.numpy as jnp
from jax import lax
from jax.experimental import pallas as pl
from jax.experimental.pallas import tpu as pltpu
from jax.sharding import PartitionSpec as P

beta_first = 0.9
beta_second = 0.95
adam_eps = 1e-08
capacity = 16
vmem_limit = 24 * 1024 * 1024


def partners(swap_pairs, count):
    slot_ids = jnp.arange(count, dtype=jnp.int32)
    pair_left = swap_pairs[:, 0:1]
    pair_right = swap_pairs[:, 1:2]
    offsets = jnp.where(pair_left == slot_ids[None, :], pair_right - slot_ids[None, :], 0)
    offsets = offsets + jnp.where(pair_right == slot_ids[None, :], pair_left - slot_ids[None, :], 0)
    return slot_ids + jnp.sum(offsets, axis=0)


def to_tiles(array, pieces):
    rows, columns = array.shape
    tiles = array.reshape(rows // 8, 8, columns // 128, 128).transpose(0, 2, 1, 3)
    return tiles.reshape(pieces, -1, 8, 128)


def from_tiles(tiles, rows, columns):
    split = tiles.reshape(rows // 8, columns // 128, 8, 128).transpose(0, 2, 1, 3)
    return split.reshape(rows, columns)


def exchange(array):
    return lax.all_to_all(array, "expert", split_axis=0, concat_axis=0, tiled=True)


def adam_update(first_in, second_in, grad):
    first_moment = beta_first * first_in.astype(jnp.float32) + (1.0 - beta_first) * grad
    second_moment = beta_second * second_in.astype(jnp.float32) + (1.0 - beta_second) * grad * grad
    direction = first_moment / (jnp.sqrt(second_moment) + adam_eps)
    return (
        first_moment.astype(jnp.bfloat16),
        second_moment.astype(jnp.bfloat16),
        direction.astype(jnp.bfloat16),
    )


def pack_kernel(
    replica_ref,
    routes_hbm,
    gates_hbm,
    tokens_hbm,
    cotangent_hbm,
    gate_ref,
    up_ref,
    down_ref,
    first_ref,
    second_ref,
    out_ref,
    weigh_ref,
    routes_ref,
    gates_ref,
    tokens_ref,
    cotangent_ref,
    rank_ref,
    weight_ref,
    row_sems,
    in_sems,
):
    count, tok = rank_ref.shape
    rows_in = [
        pltpu.make_async_copy(source, target, row_sems.at[n])
        for n, (source, target) in enumerate(
            (
                (routes_hbm, routes_ref),
                (gates_hbm, gates_ref),
                (tokens_hbm, tokens_ref),
                (cotangent_hbm, cotangent_ref),
            )
        )
    ]
    for copy in rows_in:
        copy.start()
    rows_tiles = capacity * tokens_ref.shape[1] // 1024
    state_tiles = out_ref.shape[1] - 2 * rows_tiles
    dests = 32
    replica = replica_ref[0]

    loads = []

    def load(source, slot, size):
        loads.append(
            pltpu.make_async_copy(
                source, out_ref.at[:, slot : slot + size], in_sems.at[len(loads)]
            )
        )

    slot = 0
    for ref in (gate_ref, up_ref):
        tall, wide = ref.shape[1], ref.shape[2] // 2
        for a in range(tall):
            load(ref.at[:, a, pl.ds(replica * wide, wide)], slot, wide)
            slot += wide
    share = first_ref.shape[1]
    load(down_ref.at[pl.ds(replica * count, count)], slot, share)
    load(first_ref, slot + share, share)
    load(second_ref, slot + 2 * share, share)
    for copy in loads:
        copy.start()

    for copy in rows_in[:2]:
        copy.wait()
    expert_ids = lax.broadcasted_iota(jnp.int32, (count, tok), 0)
    named = jnp.zeros((count, tok), jnp.float32)
    weight = jnp.zeros((count, tok), jnp.float32)
    gates = gates_ref[...].astype(jnp.float32)
    for k in range(routes_ref.shape[0]):
        hit = routes_ref[k : k + 1, :] == expert_ids
        named = jnp.where(hit, 1.0, named)
        weight = jnp.where(hit, gates[k : k + 1, :], weight)
    earlier = lax.broadcasted_iota(jnp.int32, (tok, tok), 0) < lax.broadcasted_iota(
        jnp.int32, (tok, tok), 1
    )
    rank_all = jnp.dot(
        named.astype(jnp.bfloat16),
        jnp.where(earlier, 1.0, 0.0).astype(jnp.bfloat16),
        preferred_element_type=jnp.float32,
    )
    rank_ref[...] = jnp.where(named > 0.0, rank_all, -1.0)
    weight_ref[...] = weight
    slot_ids = lax.broadcasted_iota(jnp.int32, (capacity, tok), 0).astype(jnp.float32)
    for copy in rows_in[2:]:
        copy.wait()

    def one_step(step, carry):
        rank = rank_ref[pl.ds(pl.multiple_of(step * dests, dests), dests), :]
        weight = weight_ref[pl.ds(pl.multiple_of(step * dests, dests), dests), :]
        picks, weighs = [], []
        for s in range(dests):
            chosen = rank[s : s + 1, :] == slot_ids
            picks.append(jnp.where(chosen, 1.0, 0.0))
            weighs.append(jnp.where(chosen, weight[s : s + 1, :], 0.0))
        pick = jnp.concatenate(picks, axis=0).astype(jnp.bfloat16)
        weigh = jnp.concatenate(weighs, axis=0).astype(jnp.bfloat16)
        weigh_ref[pl.ds(pl.multiple_of(step * dests * capacity, 128), dests * capacity), :] = weigh
        for part, (lhs, rhs) in enumerate(((pick, tokens_ref), (weigh, cotangent_ref))):
            rows = jnp.dot(lhs, rhs[...], preferred_element_type=jnp.float32)
            wide = rows.shape[1] // 128
            for index in range(dests * rows_tiles):
                i, j = divmod(index, wide)
                out_ref[
                    step * dests + index // rows_tiles,
                    state_tiles + part * rows_tiles + index % rows_tiles,
                ] = rows[8 * i : 8 * i + 8, 128 * j : 128 * j + 128].astype(jnp.bfloat16)
        return carry

    lax.fori_loop(0, count // dests, one_step, 0)
    for copy in loads:
        copy.wait()


def pack(routes, route_gates, tokens, cotangent, gate_w, up_w, down_w, first, second, replica):
    count = lax.axis_size("expert")
    tok, width = tokens.shape
    share = first.size // (count * 1024)
    tiles = 5 * share + 2 * capacity * width // 1024

    def columns(array):
        wide = array.shape[1] // 128
        return to_tiles(array, count).reshape(count, -1, wide, 8, 128)

    vmem = pl.BlockSpec(memory_space=pltpu.VMEM)
    anywhere = pl.BlockSpec(memory_space=pl.ANY)
    gate_view, up_view = columns(gate_w), columns(up_w)
    return pl.pallas_call(
        pack_kernel,
        out_shape=(
            pltpu.VMEM((count, tiles, 8, 128), jnp.bfloat16),
            jax.ShapeDtypeStruct((count * capacity, tok), jnp.bfloat16),
        ),
        in_specs=[pl.BlockSpec(memory_space=pltpu.SMEM)] + [anywhere] * 9,
        out_specs=(vmem, vmem),
        scratch_shapes=[
            pltpu.VMEM(routes.shape, routes.dtype),
            pltpu.VMEM(route_gates.shape, route_gates.dtype),
            pltpu.VMEM(tokens.shape, tokens.dtype),
            pltpu.VMEM(cotangent.shape, cotangent.dtype),
            pltpu.VMEM((count, tok), jnp.float32),
            pltpu.VMEM((count, tok), jnp.float32),
            pltpu.SemaphoreType.DMA((4,)),
            pltpu.SemaphoreType.DMA((2 * gate_view.shape[1] + 3,)),
        ],
        cost_estimate=pl.CostEstimate(
            flops=4 * count * capacity * tok * width, bytes_accessed=26_000_000, transcendentals=0
        ),
        compiler_params=pltpu.CompilerParams(vmem_limit_bytes=vmem_limit),
        name="pack",
    )(
        replica,
        *[
            pltpu.with_memory_space_constraint(member, pltpu.HBM)
            for member in (
                routes,
                route_gates,
                tokens,
                cotangent,
                gate_view,
                up_view,
                to_tiles(down_w, 2 * count),
                to_tiles(first, count),
                to_tiles(second, count),
            )
        ],
    )


def split_kernel(landed_ref, x_ref, scaled_ref, state_ref, sems):
    out_tiles = x_ref.shape[1]
    state_tiles = state_ref.shape[1]
    parts = sems.shape[0]
    each = x_ref.shape[0] // parts
    copies = [
        pltpu.make_async_copy(
            landed_ref.at[part * each : (part + 1) * each, :state_tiles],
            state_ref.at[part * each : (part + 1) * each],
            sems.at[part],
        )
        for part in range(parts)
    ]
    for copy in copies:
        copy.start()

    def rows(block, carry):
        x_ref[block] = landed_ref[block, state_tiles : state_tiles + out_tiles]
        scaled_ref[block] = landed_ref[block, state_tiles + out_tiles :]
        return carry

    lax.fori_loop(0, x_ref.shape[0], rows, 0, unroll=2)
    for copy in copies:
        copy.wait()


def split(landed, out_tiles):
    count, tiles = landed.shape[:2]
    vmem = pl.BlockSpec(memory_space=pltpu.VMEM)
    rows = pltpu.VMEM((count, out_tiles, 8, 128), jnp.bfloat16)
    return pl.pallas_call(
        split_kernel,
        out_shape=(
            rows,
            rows,
            pltpu.HBM((count, tiles - 2 * out_tiles, 8, 128), jnp.bfloat16),
        ),
        in_specs=[vmem],
        out_specs=(vmem, vmem, pl.BlockSpec(memory_space=pl.ANY)),
        scratch_shapes=[pltpu.SemaphoreType.DMA((4,))],
        compiler_params=pltpu.CompilerParams(vmem_limit_bytes=vmem_limit),
        cost_estimate=pl.CostEstimate(flops=0, bytes_accessed=8_400_000, transcendentals=0),
        name="split",
    )(pltpu.with_memory_space_constraint(landed, pltpu.VMEM))


def onward_kernel(partner_ref, answer_ref, state_ref, out_ref, stage_ref, state_sems, sems):
    count, out_tiles = answer_ref.shape[:2]
    tiles = stage_ref.shape[1]

    def piece(dest):
        return pltpu.make_async_copy(
            state_ref.at[partner_ref[dest]],
            stage_ref.at[dest, out_tiles:],
            state_sems.at[dest],
        )

    def start(dest, carry):
        piece(dest).start()
        return carry

    def wait(dest, carry):
        piece(dest).wait()
        return carry

    answer = pltpu.make_async_copy(answer_ref, stage_ref.at[:, :out_tiles], sems.at[0])
    answer.start()
    lax.fori_loop(0, count, start, 0)
    answer.wait()
    lax.fori_loop(0, count, wait, 0)
    leave = pltpu.make_async_copy(stage_ref, out_ref.at[:, :tiles], sems.at[1])
    leave.start()
    leave.wait()


def pack_onward(answer, gathered, partner, state_tiles, grad_tiles):
    count, out_tiles = answer.shape[:2]
    anywhere = pl.BlockSpec(memory_space=pl.ANY)
    return pl.pallas_call(
        onward_kernel,
        out_shape=jax.ShapeDtypeStruct(
            (count, out_tiles + state_tiles + grad_tiles, 8, 128), jnp.bfloat16
        ),
        in_specs=[pl.BlockSpec(memory_space=pltpu.SMEM), anywhere, anywhere],
        out_specs=anywhere,
        scratch_shapes=[
            pltpu.VMEM((count, out_tiles + state_tiles, 8, 128), jnp.bfloat16),
            pltpu.SemaphoreType.DMA((count,)),
            pltpu.SemaphoreType.DMA((2,)),
        ],
        cost_estimate=pl.CostEstimate(flops=0, bytes_accessed=24_000_000, transcendentals=0),
        name="pack_onward",
    )(partner, answer, pltpu.with_memory_space_constraint(gathered, pltpu.HBM))


def grad_kernel(partner_ref, halves_ref, onward_ref, out_ref, stage_ref, sems):
    count, share = stage_ref.shape[:2]
    chunks = sems.shape[0]
    each = count // chunks

    def one(dest, carry):
        place = partner_ref[dest]
        total = halves_ref[place].astype(jnp.float32)
        for r in range(1, halves_ref.shape[0] // count):
            total = total + halves_ref[r * count + place].astype(jnp.float32)
        stage_ref[dest] = total.astype(jnp.bfloat16)
        return carry

    leaves = []
    for chunk in range(chunks):
        here = slice(chunk * each, (chunk + 1) * each)
        lax.fori_loop(chunk * each, (chunk + 1) * each, one, 0, unroll=4)
        leaves.append(
            pltpu.make_async_copy(
                stage_ref.at[here], out_ref.at[here, out_ref.shape[1] - share :], sems.at[chunk]
            )
        )
        leaves[-1].start()
    for leave in leaves:
        leave.wait()


def add_grad(halves, onward, partner):
    count = onward.shape[0]
    share = halves.shape[1]
    anywhere = pl.BlockSpec(memory_space=pl.ANY)
    return pl.pallas_call(
        grad_kernel,
        out_shape=jax.ShapeDtypeStruct(onward.shape, onward.dtype),
        in_specs=[
            pl.BlockSpec(memory_space=pltpu.SMEM),
            pl.BlockSpec(memory_space=pltpu.VMEM),
            anywhere,
        ],
        out_specs=anywhere,
        scratch_shapes=[
            pltpu.VMEM((count, share, 8, 128), jnp.bfloat16),
            pltpu.SemaphoreType.DMA((4,)),
        ],
        input_output_aliases={2: 0},
        cost_estimate=pl.CostEstimate(flops=0, bytes_accessed=5_000_000, transcendentals=0),
        name="add_grad",
    )(partner, pltpu.with_memory_space_constraint(halves, pltpu.VMEM), onward)


def update_kernel(
    landed_ref,
    gate_ref,
    up_ref,
    down_ref,
    first_ref,
    second_ref,
    step_ref,
    stage_ref,
    weight_sems,
    state_sems,
):
    count, share = gate_ref.shape[:2]
    slot = landed_ref.shape[1] - 6 * share
    chunks = state_sems.shape[1]
    each = count // chunks
    weights = [
        pltpu.make_async_copy(
            landed_ref.at[:, slot + n * share : slot + (n + 1) * share], target, weight_sems.at[n]
        )
        for n, target in enumerate((gate_ref, up_ref, down_ref))
    ]
    for copy in weights:
        copy.start()

    def leave(n, chunk):
        here = pl.ds(chunk * each, each)
        target = (first_ref, second_ref, step_ref)[n]
        return pltpu.make_async_copy(
            stage_ref.at[n, here], target.at[here], state_sems.at[n, chunk]
        )

    def one_piece(piece, carry):
        first_in, second_in, grad = [
            landed_ref[piece, slot + n * share : slot + (n + 1) * share] for n in (3, 4, 5)
        ]
        for n, member in enumerate(adam_update(first_in, second_in, grad.astype(jnp.float32))):
            stage_ref[n, piece] = member
        return carry

    def two_pieces(chunk):
        def both(pair, carry):
            one_piece(chunk * each + 2 * pair, carry)
            return one_piece(chunk * each + 2 * pair + 1, carry)

        return both

    def one_chunk(chunk, carry):
        lax.fori_loop(0, each // 2, two_pieces(chunk), 0)
        for n in range(3):
            leave(n, chunk).start()
        return carry

    def one_wait(chunk, carry):
        for n in range(3):
            leave(n, chunk).wait()
        return carry

    lax.fori_loop(0, chunks, one_chunk, 0)
    lax.fori_loop(0, chunks, one_wait, 0)
    for copy in weights:
        copy.wait()


def update(landed, share):
    count = landed.shape[0]
    anywhere = pl.BlockSpec(memory_space=pl.ANY)
    piece = jax.ShapeDtypeStruct((count, share, 8, 128), jnp.bfloat16)
    return pl.pallas_call(
        update_kernel,
        out_shape=(piece,) * 6,
        in_specs=[pl.BlockSpec(memory_space=pltpu.VMEM)],
        out_specs=(anywhere,) * 6,
        scratch_shapes=[
            pltpu.VMEM((3, count, share, 8, 128), jnp.bfloat16),
            pltpu.SemaphoreType.DMA((3,)),
            pltpu.SemaphoreType.DMA((3, 8)),
        ],
        compiler_params=pltpu.CompilerParams(vmem_limit_bytes=vmem_limit),
        cost_estimate=pl.CostEstimate(
            flops=20_000_000, bytes_accessed=9_500_000, transcendentals=1_600_000
        ),
        name="update",
    )(pltpu.with_memory_space_constraint(landed, pltpu.VMEM))


def local(
    tokens,
    routes,
    route_gates,
    cotangent,
    swap_pairs,
    w_gate,
    w_up,
    w_down,
    moment_first,
    moment_second,
):
    count = lax.axis_size("expert")
    replica = lax.axis_index("dp")
    tok, width = tokens.shape
    gate_w, up_w, down_w = w_gate[0], w_up[0], w_down[0]
    half = gate_w.shape[1] // lax.axis_size("dp")
    share = half * width // (count * 1024)
    out_tiles = capacity * width // 1024

    packed, weigh = pack(
        routes.T,
        route_gates.T,
        tokens,
        cotangent,
        gate_w,
        up_w,
        down_w,
        moment_first[0],
        moment_second[0],
        replica.astype(jnp.int32).reshape(1),
    )
    spread = exchange(packed)
    spread, swap_pairs, weigh = lax.optimization_barrier((spread, swap_pairs, weigh))
    partner = partners(swap_pairs, count)

    state_tiles = 5 * share
    x_tiles, scaled_tiles, state = split(spread, out_tiles)
    x_rows = from_tiles(x_tiles, count * capacity, width)
    scaled = from_tiles(scaled_tiles, count * capacity, width)
    gate_pre = jnp.dot(x_rows, gate_w, preferred_element_type=jnp.float32)
    up_pre = jnp.dot(x_rows, up_w, preferred_element_type=jnp.float32)
    hidden = (jax.nn.silu(gate_pre) * up_pre).astype(jnp.bfloat16)
    partial = lax.dot_general(
        hidden, scaled, (((0,), (0,)), ((), ())), preferred_element_type=jnp.float32
    ).astype(jnp.bfloat16)
    pieces = to_tiles(partial, lax.axis_size("dp") * count)
    halves = lax.all_to_all(pieces, ("dp", "expert"), split_axis=0, concat_axis=0, tiled=True)

    hidden, pieces = lax.optimization_barrier((hidden, pieces))
    outputs = jnp.dot(hidden, down_w, preferred_element_type=jnp.float32).astype(jnp.bfloat16)
    onward = pack_onward(to_tiles(outputs, count), state, partner, state_tiles, share)
    onward = add_grad(halves, onward, partner)
    landed = exchange(onward)

    returned = from_tiles(landed[:, :out_tiles], count * capacity, width)
    combined = lax.dot_general(
        weigh, returned, (((0,), (0,)), ((), ())), preferred_element_type=jnp.float32
    ).astype(jnp.bfloat16)
    gate_out, up_out, down_out, first_out, second_out, step_out = update(landed, share)
    return (
        combined,
        from_tiles(gate_out, width, half)[None],
        from_tiles(up_out, width, half)[None],
        from_tiles(down_out, half, width)[None],
        from_tiles(first_out, half, width)[None],
        from_tiles(second_out, half, width)[None],
        from_tiles(step_out, half, width)[None],
    )


def solution(mesh):
    placed = (
        P(("dp", "expert"), None),
        P(("dp", "expert"), None),
        P(("dp", "expert"), None),
        P(("dp", "expert"), None),
        P(),
        P("expert", None, None),
        P("expert", None, None),
        P("expert", None, None),
        P("expert", "dp", None),
        P("expert", "dp", None),
    )
    return jax.shard_map(
        local,
        mesh=mesh,
        in_specs=placed,
        out_specs=(
            P(("dp", "expert"), None),
            P("expert", None, "dp"),
            P("expert", None, "dp"),
            P("expert", "dp", None),
            P("expert", "dp", None),
            P("expert", "dp", None),
            P("expert", "dp", None),
        ),
        check_vma=False,
    )
```
